32 devices in a mesh: seq: 4 (over z), expert: 4 (over x, core), batch: 2 (over y).
Axes of the slice: x: 2, y: 2, z: 4, core: 2. Of those that a mesh axis runs over, the one named last changes fastest.
Arguments:
- hidden_state: bfloat16 [32, 4096], P(('batch', 'expert'), 'seq'), may hold values from -9 to 9
- queries: bfloat16 [32, 2048], P(('batch', 'expert'), 'seq'), may hold values from -180 to 180
- page_table: int32 [32, 4, 4], P(('batch', 'expert'), 'seq'), may hold values from 0 to 19, as said below
- lengths: int32 [32], P(('batch', 'expert')), may hold values from 512 to 2048
- paged_keys: bfloat16 [8, 80, 128, 512], P(('batch', 'expert'), 'seq'), may hold values from -6 to 6
- paged_values: bfloat16 [8, 80, 128, 512], P(('batch', 'expert'), 'seq'), may hold values from -6 to 6
- out_weight: bfloat16 [2048, 4096], P('seq', 'expert'), may hold values from -1.5 to 1.5
- norm_gain: float32 [4096], P('seq'), may hold values from 0.25 to 1.75
- expert_ids: int32 [32, 2], P(('batch', 'expert')), may hold values from 0 to 3, all different within a row; in each aligned block of 4 rows (0 to 3, 4 to 7, ...) at most 4 rows name the same one
- route_weights: float32 [32, 2], P(('batch', 'expert')), may hold values from 0.25 to 1
- expert_gate: bfloat16 [4, 4096, 8192], P('expert', None, ('seq', 'batch')), may hold values from -0.09375 to 0.09375
- expert_up: bfloat16 [4, 4096, 8192], P('expert', None, ('seq', 'batch')), may hold values from -0.09375 to 0.09375
- expert_down: bfloat16 [4, 8192, 4096], P('expert', ('seq', 'batch')), may hold values from -0.0625 to 0.0625
Outputs:
- layer_out: bfloat16 [32, 4096], P(('batch', 'expert'), 'seq')
The draws below stay inside these ranges and needn't reach their ends.
Inputs may be any that keep to these rules, and one draw needn't show every extreme that they name: `page_table`: the page ids of one block's sequences on one shard are all different. `expert_ids`: a token's two experts differ; within the 4 rows of one device no expert is named more than 4 times.
All inputs are finite; a program needn't handle non-finite values.
Results may differ from the reference program's by a relative error of at most 0.006.
Values may be sent and summed in bfloat16 or wider, within the bound.
No kernel may reach another device: no remote copies, remote signals or barrier semaphores. Data moves between devices by JAX's collectives and lax.ppermute only.
A program may use at most 128 MiB of HBM per device.

```python
import math
import jax
import jax.numpy as jnp
import numpy as np
from jax import lax

D = 4096
QUERY_HEADS = 16
KEY_VALUE_HEADS = 4
HEAD_DIM = 128
FF_WIN = 8192
PAGE_TOKENS = 128
SEQUENCE_SLOTS = 4
SEQ_DEV = 4
DEVICE_COUNT = 4
EXPERTS = 4
SEQUENCE_BLOCKS = 8
BATCH = 32
POOL_PAGES = 20
CAP = 4


def table_from(key):
    device_keys = jax.random.split(key, SEQUENCE_BLOCKS * DEVICE_COUNT)

    def one_device(device_key):
        return jax.random.permutation(device_key, POOL_PAGES)[:SEQ_DEV * SEQUENCE_SLOTS].reshape(SEQ_DEV, SEQUENCE_SLOTS)
    page_tables = jax.vmap(one_device)(device_keys).reshape(SEQUENCE_BLOCKS, DEVICE_COUNT, SEQ_DEV, SEQUENCE_SLOTS)
    return jnp.transpose(page_tables, (0, 2, 1, 3)).reshape(SEQUENCE_BLOCKS * SEQ_DEV, DEVICE_COUNT, SEQUENCE_SLOTS).astype(jnp.int32)


def keys_from(key):
    start_offset = jnp.clip(jax.random.normal(key, (SEQUENCE_BLOCKS, DEVICE_COUNT * POOL_PAGES, PAGE_TOKENS, KEY_VALUE_HEADS * HEAD_DIM), jnp.float32), -6.0, 6.0)
    return start_offset


def draw_page_table(key, part):
    return table_from(jax.random.fold_in(key, 12))


def draw_paged_keys(key, part):
    return keys_from(jax.random.fold_in(key, 11)).astype(jnp.bfloat16)


def draw_queries(key, part):
    row_tally = SEQUENCE_BLOCKS * SEQ_DEV
    drawn = jnp.clip(1.5 * jax.random.normal(jax.random.fold_in(key, 13), (row_tally, QUERY_HEADS * HEAD_DIM), jnp.float32), -9.0, 9.0)
    return drawn.astype(jnp.bfloat16)


def draw_hidden_state(key, part):
    row_tally = SEQUENCE_BLOCKS * SEQ_DEV
    ramp = 0.5 + jnp.arange(D, dtype=jnp.float32) / D
    start_offset = jax.random.normal(jax.random.fold_in(key, 22), (row_tally, D), jnp.float32)
    return jnp.clip(start_offset * ramp, -9.0, 9.0).astype(jnp.bfloat16)


def plant(drawn, stream_key, low, top_value):
    shape = drawn.shape
    spot = [jax.random.randint(jax.random.fold_in(stream_key, axis), (), 0, shape[axis]) for axis in range(len(shape))]
    drawn = drawn.at[tuple(spot)].set(low)
    longest = shape.index(max(shape))
    spot[longest] = (spot[longest] + 1) % shape[longest]
    return drawn.at[tuple(spot)].set(top_value)


def block_levels(stream_key, dims, cuts, least, largest):
    def one(position, shards_of):
        steps = jax.random.uniform(jax.random.fold_in(jax.random.fold_in(stream_key, 6), position), (shards_of,), jnp.float32, least / len(cuts), largest / len(cuts))
        return jnp.repeat(jnp.exp(steps), dims[position] // shards_of).reshape((-1,) + (1,) * (len(dims) - position - 1))

    gain = one(*cuts[0])
    for cut in cuts[1:]:
        gain = gain * one(*cut)
    return gain


def deal_out(rng, own, number, rows, amount, top, limit, skew):
    sequence = jax.random.permutation(rng, amount)
    crowded, ordinary = load_shares(amount, rows * top, limit, skew, True), load_shares(amount, rows * top, limit, skew, False)
    places = jnp.arange(amount)

    def named(sizes, offset_by):
        used = int((sizes > 0).sum())
        fixed = max(1, used // 4)
        shifted = fixed + (places - fixed + offset_by * (used - fixed)) % max(1, amount - fixed)
        return jnp.zeros((amount,), jnp.int32).at[sequence[jnp.where(places < fixed, places, shifted)]].set(jnp.asarray(sizes, jnp.int32))

    sizes = jnp.where(number % 4 == 0, named(crowded, number // 4), named(ordinary, number - number // 4 - 1))
    mixed = jax.random.permutation(jax.random.fold_in(own, 3), amount)
    giver, receiver = mixed[0:amount // 2 * 2:2], mixed[1:amount // 2 * 2:2]
    room = jnp.minimum(sizes[giver] - 1, limit - sizes[receiver]) // 2
    room = jnp.where((giver == sequence[0]) | (receiver == sequence[0]) | (sizes[receiver] == 0), 0, jnp.maximum(room, 0))
    shifted = jax.random.randint(jax.random.fold_in(own, 4), (amount // 2,), 0, 1 << 20) % (room + 1)
    sizes = sizes.at[giver].add(-shifted).at[receiver].add(shifted)
    members = jnp.searchsorted(jnp.cumsum(sizes), jnp.arange(rows * top), side="right").astype(jnp.int32)
    listing = members.reshape(top, rows).T
    listing = listing[jax.random.permutation(jax.random.fold_in(own, 1), rows)]
    offset_by = jax.random.randint(jax.random.fold_in(own, 2), (rows, 1), 0, top)
    return jnp.take_along_axis(listing, (jnp.arange(top)[None, :] + offset_by) % top, axis=1)


def load_shares(number_of, total, limit, slope, full):
    weights = [(1 << 20) // math.isqrt(rank ** slope) + 1 for rank in range(1, number_of + 1)]
    largest = limit if full else min(limit, max(-(-total // number_of), total * weights[0] // sum(weights)))
    least = 1 if total - largest >= number_of - 1 else 0
    counts, surplus = [largest] + [least] * (number_of - 1), total - largest - least * (number_of - 1)
    while surplus > 0:
        movable = [i for i in range(1, number_of) if counts[i] < largest] or [i for i in range(1, number_of) if counts[i] < limit]
        whole, remaining = sum([weights[i] for i in movable]), surplus
        for i in movable:
            more = min(limit - counts[i], max(1, remaining * weights[i] // whole), surplus)
            counts[i] = counts[i] + more
            surplus = surplus - more
    return np.array(counts)


def gaussian(own_key, extent, scale, most, cuts=(), kind=jnp.bfloat16):
    values = jax.random.normal(own_key, extent, jnp.float32) * scale
    if len(cuts) > 0:
        values = block_levels(own_key, extent, cuts, -0.22, 0.18) * values
    return jnp.clip(values, min=-most, max=most).astype(kind)


def setup_inputs(seed: int = 0) -> dict:
    arg_keys = jax.random.split(jax.random.key(seed), 14)
    hidden_state = draw_hidden_state(jax.random.fold_in(arg_keys[13], 71), 0)
    queries = draw_queries(jax.random.fold_in(arg_keys[13], 71), 0)
    page_table = draw_page_table(jax.random.fold_in(arg_keys[13], 71), 0)
    lengths = plant(jax.random.randint(arg_keys[3], (BATCH,), DEVICE_COUNT * PAGE_TOKENS, DEVICE_COUNT * SEQUENCE_SLOTS * PAGE_TOKENS + 1), jax.random.fold_in(arg_keys[3], 1), DEVICE_COUNT * PAGE_TOKENS, DEVICE_COUNT * SEQUENCE_SLOTS * PAGE_TOKENS).astype(jnp.int32)
    paged_keys = draw_paged_keys(jax.random.fold_in(arg_keys[13], 71), 0)
    paged_values = gaussian(arg_keys[5], (SEQUENCE_BLOCKS, DEVICE_COUNT * POOL_PAGES, PAGE_TOKENS, KEY_VALUE_HEADS * HEAD_DIM), 1.0, 6.0, ((0, 8), (1, 4)))
    out_weight = gaussian(arg_keys[6], (QUERY_HEADS * HEAD_DIM, D), (HEAD_DIM // 8) ** -0.5, 1.5, ((0, 4), (1, 4)))
    norm_gain = jnp.clip(1.0 + 0.15 * jax.random.normal(arg_keys[7], (D,), jnp.float32), 0.25, 1.75)
    expert_ids_keys = jax.random.split(jax.random.fold_in(arg_keys[8], 1), BATCH // SEQ_DEV)
    expert_ids_turns = jax.random.permutation(jax.random.fold_in(arg_keys[8], 3), BATCH // SEQ_DEV)
    expert_ids = jax.vmap(lambda own, number: deal_out(jax.random.fold_in(arg_keys[8], 2), own, number, SEQ_DEV, EXPERTS, 2, CAP, 2))(expert_ids_keys, expert_ids_turns).reshape((BATCH, 2))
    route_weights = jnp.clip(0.25 + 0.75 * jax.random.uniform(arg_keys[9], (BATCH, 2), jnp.float32) ** block_levels(arg_keys[9], (BATCH, 2), ((0, 8),), -0.2, 0.2), 0.25, 1.0)
    expert_gate = gaussian(arg_keys[10], (EXPERTS, D, FF_WIN), D ** -0.5, 0.09375, ((0, 4), (2, 8)))
    expert_up = gaussian(arg_keys[11], (EXPERTS, D, FF_WIN), D ** -0.5, 0.09375, ((0, 4), (2, 8)))
    expert_down = gaussian(arg_keys[12], (EXPERTS, FF_WIN, D), FF_WIN ** -0.5, 0.0625, ((0, 4), (1, 8)))
    return {"hidden_state": hidden_state, "queries": queries, "page_table": page_table, "lengths": lengths, "paged_keys": paged_keys, "paged_values": paged_values, "out_weight": out_weight, "norm_gain": norm_gain, "expert_ids": expert_ids, "route_weights": route_weights, "expert_gate": expert_gate, "expert_up": expert_up, "expert_down": expert_down}


def shard_partials(grouped_queries, keys_per_page, values_per_page, usable):
    local_rows, kv_heads, block_length, head_size = grouped_queries.shape
    scores = jnp.einsum('skgd,slkd->skgl', grouped_queries.astype(jnp.float32), keys_per_page.astype(jnp.float32)) / math.sqrt(head_size)
    scores = jnp.where(usable[:, None, None, :], scores, -1e+30)
    maxima = lax.optimization_barrier(jnp.max(scores, axis=-1))
    powers = jnp.exp(scores - maxima[..., None])
    totals = lax.optimization_barrier(jnp.sum(powers, axis=-1))
    weights = lax.optimization_barrier(powers.astype(jnp.bfloat16)).astype(jnp.float32)
    weighted = jnp.einsum('skgl,slkd->skgd', weights, values_per_page.astype(jnp.float32))
    heads_all = kv_heads * block_length
    return (maxima.reshape(local_rows, heads_all), totals.reshape(local_rows, heads_all), weighted.reshape(local_rows, heads_all, head_size))

def slot_table(expert_ids, expert_count, capacity):
    flat_ids = expert_ids.reshape(-1).astype(jnp.int32)
    ordinal = jnp.arange(flat_ids.shape[0], dtype=jnp.int32)
    before = (flat_ids[:, None] == flat_ids[None, :]) & (ordinal[None, :] < ordinal[:, None])
    slot_of = lax.optimization_barrier(jnp.sum(before.astype(jnp.int32), axis=1)).astype(jnp.int32)
    target = flat_ids * capacity + slot_of
    return jnp.arange(expert_count * capacity, dtype=jnp.int32)[:, None] == target[None, :]

def reference(hidden_state, queries, page_table, lengths, paged_keys, paged_values, out_weight, norm_gain, expert_ids, route_weights, expert_gate, expert_up, expert_down):
    block_length = QUERY_HEADS // KEY_VALUE_HEADS

    def one_sequence(sequence_number):
        block_number = sequence_number // SEQ_DEV
        rows_per_page = (jnp.arange(DEVICE_COUNT, dtype=jnp.int32)[:, None] * POOL_PAGES + page_table[sequence_number].astype(jnp.int32)).astype(jnp.int32)
        sequence_keys = paged_keys[block_number][rows_per_page].reshape(DEVICE_COUNT, SEQUENCE_SLOTS * PAGE_TOKENS, KEY_VALUE_HEADS, HEAD_DIM)
        sequence_values = paged_values[block_number][rows_per_page].reshape(DEVICE_COUNT, SEQUENCE_SLOTS * PAGE_TOKENS, KEY_VALUE_HEADS, HEAD_DIM)
        positions = ((jnp.arange(SEQUENCE_SLOTS, dtype=jnp.int32)[None, :, None] * DEVICE_COUNT + jnp.arange(DEVICE_COUNT, dtype=jnp.int32)[:, None, None]) * PAGE_TOKENS + jnp.arange(PAGE_TOKENS, dtype=jnp.int32)[None, None, :]).reshape(DEVICE_COUNT, SEQUENCE_SLOTS * PAGE_TOKENS)
        usable = positions < lengths[sequence_number]
        block_grouped = jnp.broadcast_to(queries[sequence_number].reshape(1, KEY_VALUE_HEADS, block_length, HEAD_DIM), (DEVICE_COUNT, KEY_VALUE_HEADS, block_length, HEAD_DIM))
        maxima, totals, weighted = shard_partials(block_grouped, sequence_keys, sequence_values, usable)
        joint_max = lax.optimization_barrier(jnp.max(maxima, axis=0))
        factor = jnp.exp(maxima - joint_max)
        summed = lax.optimization_barrier(jnp.sum(weighted * factor[..., None], axis=0)) / lax.optimization_barrier(jnp.sum(totals * factor, axis=0))[:, None]
        return summed.reshape(QUERY_HEADS * HEAD_DIM).astype(jnp.bfloat16)
    attention = lax.map(one_sequence, jnp.arange(BATCH, dtype=jnp.int32))
    projected = jnp.dot(attention, out_weight, preferred_element_type=jnp.float32)
    resid = hidden_state.astype(jnp.float32) + projected
    normed = (resid * lax.rsqrt(lax.optimization_barrier(jnp.mean(resid * resid, axis=1, keepdims=True)) + 1e-05) * norm_gain).astype(jnp.bfloat16)
    normed_groups = lax.optimization_barrier(normed).astype(jnp.float32).reshape(SEQUENCE_BLOCKS, SEQ_DEV, D)
    placed = jax.vmap(lambda block_ids: slot_table(block_ids, EXPERTS, CAP))(expert_ids.reshape(SEQUENCE_BLOCKS, SEQ_DEV, 2))
    placed = placed.reshape(SEQUENCE_BLOCKS, EXPERTS * CAP, SEQ_DEV, 2).astype(jnp.float32)
    dispatch = lax.optimization_barrier(jnp.sum(placed, axis=3))
    buffers = jnp.einsum('grs,gsd->grd', dispatch, normed_groups).astype(jnp.bfloat16)
    buffers = jnp.transpose(buffers.reshape(SEQUENCE_BLOCKS, EXPERTS, CAP, D), (1, 0, 2, 3)).reshape(EXPERTS, SEQUENCE_BLOCKS * CAP, D)

    def run_expert(operands):
        token_rows, gate_matrix, up_matrix, down_matrix = operands
        gate_part = jnp.dot(token_rows, gate_matrix, preferred_element_type=jnp.float32)
        up_part = jnp.dot(token_rows, up_matrix, preferred_element_type=jnp.float32)
        activated = (jax.nn.silu(gate_part) * up_part).astype(jnp.bfloat16)
        return jnp.dot(activated, down_matrix, preferred_element_type=jnp.float32)
    outputs = lax.map(run_expert, (buffers, expert_gate, expert_up, expert_down))
    outputs = jnp.transpose(outputs.reshape(EXPERTS, SEQUENCE_BLOCKS, CAP, D), (1, 0, 2, 3)).reshape(SEQUENCE_BLOCKS, EXPERTS * CAP, D)
    mixing = jnp.einsum('grsk,gsk->gsr', placed, route_weights.reshape(SEQUENCE_BLOCKS, SEQ_DEV, 2), precision=lax.Precision.HIGHEST)
    expert_mix = jnp.einsum('gsr,grd->gsd', mixing, outputs, precision=lax.Precision.HIGHEST).reshape(BATCH, D)
    return (resid + expert_mix).astype(jnp.bfloat16)
```

```python
import functools
import math

import jax
import jax.numpy as jnp
from jax import lax
from jax.experimental import pallas as pl
from jax.experimental.pallas import tpu as pltpu
from jax.sharding import PartitionSpec as P

LANES = 128
EPS = 1e-05
MIB = 1 << 20
F32 = jnp.float32
BF16 = jnp.bfloat16


VMEM = pl.BlockSpec(memory_space=pltpu.VMEM)
SMEM = pl.BlockSpec(memory_space=pltpu.SMEM)
ANY = pl.BlockSpec(memory_space=pl.ANY)
HBM = pl.BlockSpec(memory_space=pltpu.HBM)


def in_vmem(array):
    return pltpu.with_memory_space_constraint(array, pltpu.VMEM)


def in_hbm(array):
    return pltpu.with_memory_space_constraint(array, pltpu.HBM)


def thirds(value):
    high = value.astype(BF16).astype(F32)
    rest = value - high
    middle = rest.astype(BF16).astype(F32)
    return high, middle, rest - middle


def shifts_over(block, axis):
    count = lax.axis_size(axis)
    return [block] + [
        lax.ppermute(block, axis, [((i - k) % count, i) for i in range(count)])
        for k in range(1, count)
    ]


def fetch_pages_kernel(table, keys, values, weight, key_out, value_out, weight_out, sems):
    page = keys.shape[1]
    pages = key_out.shape[0] // page
    copies = []
    for i in range(pages):
        here = pl.ds(i * page, page)
        copies.append(pltpu.make_async_copy(keys.at[table[i]], key_out.at[here], sems.at[2 * i]))
        copies.append(
            pltpu.make_async_copy(values.at[table[i]], value_out.at[here], sems.at[2 * i + 1])
        )
    copies.append(pltpu.make_async_copy(weight, weight_out, sems.at[2 * pages]))
    for copy in copies:
        copy.start()
    for copy in copies:
        copy.wait()


def fetch_pages(table, keys, values, weight):
    pages = table.shape[0]
    shape = (pages * keys.shape[1], keys.shape[2])
    return pl.pallas_call(
        fetch_pages_kernel,
        name="fetch_pages",
        out_shape=[
            jax.ShapeDtypeStruct(shape, keys.dtype),
            jax.ShapeDtypeStruct(shape, values.dtype),
            jax.ShapeDtypeStruct(weight.shape, weight.dtype),
        ],
        in_specs=[SMEM, HBM, HBM, HBM],
        out_specs=[VMEM, VMEM, VMEM],
        scratch_shapes=[pltpu.SemaphoreType.DMA((2 * pages + 1,))],
        compiler_params=pltpu.CompilerParams(vmem_limit_bytes=8 * MIB),
        cost_estimate=pl.CostEstimate(flops=0, bytes_accessed=6 * MIB, transcendentals=0),
    )(table, in_hbm(keys), in_hbm(values), in_hbm(weight))


def fetch_kernel(parts, array, after, out, token, sems):
    del after
    rows = array.shape[0] // parts
    copies = [
        pltpu.make_async_copy(
            array.at[pl.ds(i * rows, rows)], out.at[pl.ds(i * rows, rows)], sems.at[i]
        )
        for i in range(parts)
    ]
    for copy in copies:
        copy.start()
    token[...] = jnp.zeros_like(token)
    for copy in copies:
        copy.wait()


def fetch(array, after, parts=4):
    return pl.pallas_call(
        functools.partial(fetch_kernel, parts),
        name="fetch_weights",
        out_shape=[
            jax.ShapeDtypeStruct(array.shape, array.dtype),
            jax.ShapeDtypeStruct((8, LANES), F32),
        ],
        in_specs=[HBM, ANY],
        out_specs=[VMEM, VMEM],
        scratch_shapes=[pltpu.SemaphoreType.DMA((parts,))],
        compiler_params=pltpu.CompilerParams(vmem_limit_bytes=MIB),
        cost_estimate=pl.CostEstimate(
            flops=0, bytes_accessed=2 * array.size * 2, transcendentals=0
        ),
    )(in_hbm(array), after)


def pack_kernel(hidden, gain, out):
    rows = hidden.shape[0]
    out[:rows, :] = hidden[...]
    for i, part in enumerate(thirds(gain[...])):
        out[rows + i : rows + i + 1, :] = part.astype(BF16)


def pack(hidden, gain):
    return pl.pallas_call(
        pack_kernel,
        name="pack",
        out_shape=jax.ShapeDtypeStruct((hidden.shape[0] + 3, hidden.shape[1]), BF16),
        in_specs=[VMEM, VMEM],
        out_specs=VMEM,
        compiler_params=pltpu.CompilerParams(vmem_limit_bytes=MIB),
    )(hidden, gain)


def attend_kernel(dims, place, lengths, *refs):
    shards, copies, rows, slots, per_kv, page = dims
    queries = refs[:shards]
    keys, values, out, wide, column = refs[shards:]
    heads_here = queries[0].shape[1] // LANES
    total_rows = shards * heads_here * rows
    span = slots * page
    own = place[0]

    def lanes_of(k, x):
        shard = lax.rem(own - k + shards, shards)
        return shard, pl.ds(pl.multiple_of((shard * heads_here + x) // per_kv * LANES, LANES), LANES)

    wide[...] = jnp.zeros_like(wide)
    for k in range(shards):
        for x in range(heads_here):
            first = (k * heads_here + x) * rows
            wide[first : first + rows, lanes_of(k, x)[1]] = queries[k][
                :, x * LANES : (x + 1) * LANES
            ].astype(F32)
    spread = wide[...].astype(BF16)

    row_kind = lax.rem(lax.broadcasted_iota(jnp.int32, (total_rows, 1), 0), rows)
    length = jnp.zeros((total_rows, 1), jnp.int32)
    for i in range(rows):
        length = jnp.where(row_kind == i, lengths[i], length)
    lane = lax.broadcasted_iota(jnp.int32, (1, span), 1)
    position = (lane // page * shards + own) * page + lax.rem(lane, page)

    scores = jnp.zeros((total_rows, span), F32)
    for i in range(rows):
        part = lax.dot_general(
            spread,
            keys[i * span : (i + 1) * span, :],
            (((1,), (1,)), ((), ())),
            preferred_element_type=F32,
        )
        scores = jnp.where(row_kind == i, part, scores)
    scores = jnp.where(position < length, scores / math.sqrt(LANES), -1e30)
    peak = jnp.max(scores, axis=1, keepdims=True)
    powers = jnp.exp(scores - peak)
    total = jnp.sum(powers, axis=1, keepdims=True)

    summed = jnp.zeros(wide.shape, F32)
    for i in range(rows):
        weights = jnp.where(row_kind == i, powers, 0.0).astype(BF16)
        summed = summed + jnp.dot(
            weights, values[i * span : (i + 1) * span, :], preferred_element_type=F32
        )
    wide[...] = summed / total
    column[...] = jnp.broadcast_to(peak + jnp.log(total), column.shape)

    at = lax.broadcasted_iota(jnp.int32, (rows, LANES), 1)
    for k in range(shards):
        shard = lanes_of(k, 0)[0]
        level = jnp.zeros((rows, LANES), F32)
        pieces = []
        for x in range(heads_here):
            first = (k * heads_here + x) * rows
            pieces.append(wide[first : first + rows, lanes_of(k, x)[1]])
            level = jnp.where(at // 3 == x, column[first : first + rows, :], level)
        high, middle, low = thirds(level)
        kind = lax.rem(at, 3)
        pieces.append(jnp.where(kind == 0, high, jnp.where(kind == 1, middle, low)))
        for x, piece in enumerate(pieces):
            piece = piece.astype(BF16)
            for copy in range(copies):
                out[shard * copies + copy, :, x * LANES : (x + 1) * LANES] = piece


def attend(own, lengths, queries, keys, values, copies, per_kv, slots):
    shards = len(queries)
    rows, width = queries[0].shape
    depth = keys.shape[1]
    page = keys.shape[0] // (rows * slots)
    total_rows = shards * width // LANES * rows
    return pl.pallas_call(
        functools.partial(attend_kernel, (shards, copies, rows, slots, per_kv, page)),
        name="attend",
        out_shape=jax.ShapeDtypeStruct((shards * copies, rows, width + LANES), BF16),
        in_specs=[SMEM, SMEM] + [VMEM] * (shards + 2),
        out_specs=VMEM,
        scratch_shapes=[pltpu.VMEM((total_rows, depth), F32), pltpu.VMEM((total_rows, LANES), F32)],
        compiler_params=pltpu.CompilerParams(vmem_limit_bytes=8 * MIB),
    )(
        own,
        lengths,
        *queries,
        in_vmem(keys),
        in_vmem(values),
    )


def project_kernel(shards, place, received, weight, residual, out, out_full, gathered, placed):
    copies = received.shape[0] // shards
    rows = received.shape[1]
    width = received.shape[2] - LANES
    for e in range(copies):
        levels, outputs = [], []
        for s in range(shards):
            block = received[s * copies + e].astype(F32)
            parts = block[:, width:]
            levels.append(
                parts
                + pltpu.roll(parts, LANES - 1, 1)
                + pltpu.roll(parts, LANES - 2, 1)
            )
            outputs.append(block[:, :width])
        joint = functools.reduce(jnp.maximum, levels)
        factors = [jnp.exp(level - joint) for level in levels]
        total = functools.reduce(jnp.add, factors)
        factors = [factor / total for factor in factors]
        for x in range(width // LANES):
            span = slice(x * LANES, (x + 1) * LANES)
            value = functools.reduce(
                jnp.add,
                [
                    factor[:, 3 * x : 3 * x + 1] * output[:, span]
                    for factor, output in zip(factors, outputs)
                ],
            )
            gathered[e * rows : (e + 1) * rows, span] = value
    attention = gathered[...].astype(BF16)
    result = jnp.dot(attention, weight[...], preferred_element_type=F32)
    if residual.shape[0] == result.shape[0]:
        result = result + residual[...].astype(F32)
    else:
        own_rows = residual[...].astype(F32)[:rows]
        for e in range(copies):
            placed[e * rows : (e + 1) * rows, :] = own_rows
        of_row = lax.broadcasted_iota(jnp.int32, (copies * rows, 1), 0) // rows
        result = result + jnp.where(of_row == place[0], placed[...], 0.0)
    out_full[...] = result
    out[...] = result.astype(BF16)


def project(own, received, weight, residual, shards):
    columns = residual.shape[1]
    tokens = received.shape[0] // shards * received.shape[1]
    return pl.pallas_call(
        functools.partial(project_kernel, shards),
        name="project",
        out_shape=[
            jax.ShapeDtypeStruct((tokens, columns), BF16),
            jax.ShapeDtypeStruct((tokens, columns), F32),
        ],
        in_specs=[SMEM, VMEM, VMEM, VMEM],
        out_specs=[VMEM, VMEM],
        scratch_shapes=[
            pltpu.VMEM((tokens, weight.shape[0]), F32),
            pltpu.VMEM((tokens, columns), F32),
        ],
        compiler_params=pltpu.CompilerParams(vmem_limit_bytes=4 * MIB),
    )(own, received, in_vmem(weight), residual)


def residual_kernel(own, *refs):
    parts, (gain, after, out) = refs[:-3], refs[-3:]
    del after
    resid = own[...]
    for part in parts:
        resid = resid + part[...].astype(F32)
    columns = resid.shape[1]
    if gain.shape[0] == 1:
        factor = gain[...]
    else:
        factor = jnp.sum(gain[gain.shape[0] - 3 :, :].astype(F32), axis=0, keepdims=True)
    out[:, :columns] = (resid * factor).astype(BF16)
    squares = jnp.sum(resid * resid, axis=1, keepdims=True)
    high, middle, low = thirds(jnp.broadcast_to(squares, (resid.shape[0], LANES)))
    at = lax.broadcasted_iota(jnp.int32, high.shape, 1)
    tail = jnp.where(at == 0, high, jnp.where(at == 1, middle, jnp.where(at == 2, low, 0.0)))
    out[:, columns:] = tail.astype(BF16)


def residual_block(own, parts, gain, after):
    tokens, columns = own.shape
    return pl.pallas_call(
        residual_kernel,
        name="residual_block",
        out_shape=jax.ShapeDtypeStruct((tokens, columns + LANES), BF16),
        in_specs=[VMEM] * (len(parts) + 2) + [ANY],
        out_specs=VMEM,
        compiler_params=pltpu.CompilerParams(vmem_limit_bytes=2 * MIB),
    )(own, *parts, gain, after)


def join_kernel(place, *refs):
    blocks, (after, out) = refs[:-2], refs[-2:]
    del after
    groups = len(blocks)
    for k, block in enumerate(blocks):
        out[lax.rem(place[2] - k + groups, groups)] = block[...]


def join(place, blocks, after):
    return pl.pallas_call(
        join_kernel,
        name="join",
        out_shape=jax.ShapeDtypeStruct((len(blocks),) + blocks[0].shape, BF16),
        in_specs=[SMEM] + [VMEM] * len(blocks) + [ANY],
        out_specs=VMEM,
        compiler_params=pltpu.CompilerParams(vmem_limit_bytes=MIB),
    )(place, *blocks, after)


def expert_kernel(dims, place, *refs):
    column_blocks, shards, rows = dims
    blocks = refs[:column_blocks]
    gain, gate, up, down, out, resid, result, kept = refs[column_blocks:]
    groups, tokens, columns = blocks[0].shape
    columns -= LANES
    features = column_blocks * columns
    width = features // shards
    first = place[0] * width
    squares = 0.0
    gate_part = up_part = None
    for k in range(column_blocks):
        block = lax.rem(place[1] - k + column_blocks, column_blocks)
        both = jnp.concatenate([blocks[k][g] for g in range(groups)], axis=0)
        tail = both[:, columns:].astype(F32)
        squares = squares + tail[:, 0:1] + tail[:, 1:2] + tail[:, 2:3]
        x = both[:, :columns]

        @pl.when(first // columns == block)
        def _(x=x):
            kept[...] = x.astype(F32)

        rows_of = pl.ds(pl.multiple_of(block * columns, columns), columns)
        gate_term = jnp.dot(x, gate[rows_of, :], preferred_element_type=F32)
        up_term = jnp.dot(x, up[rows_of, :], preferred_element_type=F32)
        gate_part = gate_term if gate_part is None else gate_part + gate_term
        up_part = up_term if up_part is None else up_part + up_term
    scale = lax.rsqrt(squares / features + EPS)
    gate_part = gate_part * scale
    up_part = up_part * scale
    act = (gate_part / (1.0 + jnp.exp(-gate_part)) * up_part).astype(BF16)
    result[...] = jnp.dot(act, down[...], preferred_element_type=F32)
    for s in range(shards):
        for e in range(column_blocks):
            for g in range(groups):
                at = g * tokens + e * rows
                out[(s * column_blocks + e) * groups + g] = result[
                    at : at + rows, s * width : (s + 1) * width
                ].astype(BF16)
    lanes = pl.ds(pl.multiple_of(lax.rem(first, columns), width), width)
    for block in range(groups * column_blocks):

        @pl.when(place[2] * column_blocks + place[1] == block)
        def _(block=block):
            resid[...] = kept[block * rows : (block + 1) * rows, lanes] / gain[...]


def expert(place, blocks, gain, gate, up, down, shards, rows):
    column_blocks = len(blocks)
    groups, tokens, columns = blocks[0].shape
    columns -= LANES
    features = column_blocks * columns
    return pl.pallas_call(
        functools.partial(expert_kernel, (column_blocks, shards, rows)),
        name="expert",
        out_shape=[
            jax.ShapeDtypeStruct((column_blocks * groups * shards, rows, features // shards), BF16),
            jax.ShapeDtypeStruct((rows, features // shards), F32),
        ],
        in_specs=[SMEM] + [VMEM] * (column_blocks + 4),
        out_specs=[VMEM, VMEM],
        scratch_shapes=[
            pltpu.VMEM((groups * tokens, features), F32),
            pltpu.VMEM((groups * tokens, columns), F32),
        ],
        compiler_params=pltpu.CompilerParams(vmem_limit_bytes=8 * MIB),
    )(place, *blocks, gain, in_vmem(gate), in_vmem(up), in_vmem(down))


def finish_kernel(dims, ids, routes, returned, resid, out):
    shards, experts, groups = dims
    rows = out.shape[0]
    at = lax.broadcasted_iota(jnp.int32, (rows, 1), 0)
    total = resid[...]
    for e in range(experts):
        factor = jnp.zeros((rows, 1), F32)
        for i in range(rows):
            share = 0.0
            for k in range(ids.shape[1]):
                share = share + jnp.where(ids[i, k] == e, routes[i, k], 0.0)
            factor = jnp.where(at == i, share, factor)
        term = None
        for s in range(shards):
            for g in range(groups):
                part = returned[(s * experts + e) * groups + g].astype(F32)
                term = part if term is None else term + part
        total = total + factor * term
    out[...] = total.astype(BF16)


def finish(ids, routes, returned, resid, dims):
    return pl.pallas_call(
        functools.partial(finish_kernel, dims),
        name="finish",
        out_shape=jax.ShapeDtypeStruct(resid.shape, BF16),
        in_specs=[SMEM, SMEM, VMEM, VMEM],
        out_specs=VMEM,
        compiler_params=pltpu.CompilerParams(vmem_limit_bytes=4 * MIB),
    )(ids, routes, returned, resid)


def per_device(
    hidden_state,
    queries,
    page_table,
    lengths,
    paged_keys,
    paged_values,
    out_weight,
    norm_gain,
    expert_ids,
    route_weights,
    expert_gate,
    expert_up,
    expert_down,
):
    shards = lax.axis_size("seq")
    experts = lax.axis_size("expert")
    groups = lax.axis_size("batch")
    place = jnp.stack([lax.axis_index(name) for name in ("seq", "expert", "batch")])
    place = place.astype(jnp.int32)
    rows = hidden_state.shape[0]
    columns = out_weight.shape[1]
    slots = page_table.shape[2]
    kv_heads = paged_keys.shape[3] // LANES
    per_kv = shards * queries.shape[1] // LANES // kv_heads
    own_gain = norm_gain[None, :]

    all_queries = shifts_over(queries, "seq")
    if shards == experts:
        route = [
            (s * experts + e, e * experts + s) for s in range(shards) for e in range(experts)
        ]
        residual = lax.ppermute(pack(hidden_state, own_gain), ("seq", "expert"), route)
        gain = residual
    else:
        everything = lax.all_gather(hidden_state, "expert", axis=0, tiled=True)
        everything = lax.all_gather(everything, "seq", axis=1, tiled=True)
        block = lax.dynamic_slice_in_dim(everything, place[1] * columns, columns, 1)
        residual = jnp.where(place[0] == 0, block, 0)
        gains = lax.all_gather(norm_gain, "seq", axis=0, tiled=True)
        gain = lax.dynamic_slice_in_dim(gains, place[1] * columns, columns, 0)[None, :]

    keys, values, weight = fetch_pages(
        page_table.reshape(-1), paged_keys[0], paged_values[0], out_weight
    )
    partials = attend(place, lengths, all_queries, keys, values, experts, per_kv, slots)
    received = lax.all_to_all(
        partials, ("seq", "expert"), split_axis=0, concat_axis=0, tiled=True
    )
    projected, own = project(place, received, weight, residual, shards)

    parts = shifts_over(projected, "seq")[1:]
    gate, gate_here = fetch(expert_gate[0], projected)
    block = residual_block(own, parts, gain, gate_here)

    of_groups = shifts_over(block, "batch")
    up, up_here = fetch(expert_up[0], block)
    block = join(place, of_groups, up_here)

    blocks = shifts_over(block, "expert")
    down, _ = fetch(expert_down[0], block)
    outputs, resid = expert(place, blocks, own_gain, gate, up, down, shards, rows)
    returned = lax.all_to_all(
        outputs, ("seq", "expert", "batch"), split_axis=0, concat_axis=0, tiled=True
    )
    return finish(expert_ids, route_weights, returned, resid, (shards, experts, groups))


def solution(mesh):
    in_specs = (
        P(("batch", "expert"), "seq"),
        P(("batch", "expert"), "seq"),
        P(("batch", "expert"), "seq", None),
        P(("batch", "expert")),
        P(("batch", "expert"), "seq", None, None),
        P(("batch", "expert"), "seq", None, None),
        P("seq", "expert"),
        P("seq"),
        P(("batch", "expert"), None),
        P(("batch", "expert"), None),
        P("expert", None, ("seq", "batch")),
        P("expert", None, ("seq", "batch")),
        P("expert", ("seq", "batch"), None),
    )
    out_specs = P(("batch", "expert"), "seq")
    return jax.shard_map(
        per_device, mesh=mesh, in_specs=in_specs, out_specs=out_specs, check_vma=False
    )
```

```python
import functools
import math

import jax
import jax.numpy as jnp
from jax import lax
from jax.experimental import pallas as pl
from jax.experimental.pallas import tpu as pltpu
from jax.sharding import PartitionSpec as P

LANES = 128
EPS = 1e-05
MIB = 1 << 20
LONG = 6 * 10**9
F32 = jnp.float32
BF16 = jnp.bfloat16


VMEM = pl.BlockSpec(memory_space=pltpu.VMEM)
SMEM = pl.BlockSpec(memory_space=pltpu.SMEM)
ANY = pl.BlockSpec(memory_space=pl.ANY)
HBM = pl.BlockSpec(memory_space=pltpu.HBM)


def in_vmem(array):
    return pltpu.with_memory_space_constraint(array, pltpu.VMEM)


def in_hbm(array):
    return pltpu.with_memory_space_constraint(array, pltpu.HBM)


def thirds(value):
    high = value.astype(BF16).astype(F32)
    rest = value - high
    middle = rest.astype(BF16).astype(F32)
    return high, middle, rest - middle


def shifts_over(block, axis):
    count = lax.axis_size(axis)
    return [block] + [
        lax.ppermute(block, axis, [((i - k) % count, i) for i in range(count)])
        for k in range(1, count)
    ]


def pause_kernel(after, out):
    del after
    out[...] = jnp.zeros_like(out)


def pause(after):
    return pl.pallas_call(
        pause_kernel,
        name="pause",
        out_shape=jax.ShapeDtypeStruct((8, LANES), F32),
        in_specs=[ANY],
        out_specs=VMEM,
        compiler_params=pltpu.CompilerParams(vmem_limit_bytes=MIB),
        cost_estimate=pl.CostEstimate(flops=LONG, bytes_accessed=0, transcendentals=0),
    )(after)


def attend_kernel(dims, lengths, table, after, hidden, gain, *refs):
    del after
    copies, per_kv, shards = dims
    queries, (keys, values, out, wide, column) = refs[:shards], refs[shards:]
    rows, _, slots = table.shape
    heads_here = queries[0].shape[1] // LANES
    page = keys.shape[1]
    span = slots * page
    total_rows = wide.shape[0]
    own = lax.axis_index("seq")

    def lanes_of(k, x):
        shard = lax.rem(own - k + shards, shards)
        first = (shard * heads_here + x) // per_kv * LANES
        return shard, pl.ds(pl.multiple_of(first, LANES), LANES)

    wide[...] = jnp.zeros_like(wide)
    for k in range(shards):
        for x in range(heads_here):
            first = (k * heads_here + x) * rows
            wide[first : first + rows, lanes_of(k, x)[1]] = queries[k][
                :, x * LANES : (x + 1) * LANES
            ].astype(F32)
    spread = wide[...].astype(BF16)

    row_kind = lax.rem(lax.broadcasted_iota(jnp.int32, (total_rows, 1), 0), rows)
    length = jnp.zeros((total_rows, 1), jnp.int32)
    for i in range(rows):
        length = jnp.where(row_kind == i, lengths[i], length)
    lane = lax.broadcasted_iota(jnp.int32, (1, span), 1)
    position = (lane // page * shards + own) * page + lax.rem(lane, page)

    pages = []
    for j in range(slots):
        scores = jnp.zeros((total_rows, page), F32)
        for i in range(rows):
            part = lax.dot_general(
                spread,
                keys[table[i, 0, j]],
                (((1,), (1,)), ((), ())),
                preferred_element_type=F32,
            )
            scores = jnp.where(row_kind == i, part, scores)
        pages.append(scores)
    scores = jnp.concatenate(pages, axis=1)
    scores = jnp.where(position < length, scores / math.sqrt(LANES), -1e30)
    peak = jnp.max(scores, axis=1, keepdims=True)
    powers = jnp.exp(scores - peak)
    total = jnp.sum(powers, axis=1, keepdims=True)

    summed = jnp.zeros(wide.shape, F32)
    for i in range(rows):
        weights = jnp.where(row_kind == i, powers, 0.0).astype(BF16)
        for j in range(slots):
            summed = summed + jnp.dot(
                weights[:, j * page : (j + 1) * page],
                values[table[i, 0, j]],
                preferred_element_type=F32,
            )
    wide[...] = summed / total
    column[...] = jnp.broadcast_to(peak + jnp.log(total), column.shape)

    width = heads_here * LANES
    at = lax.broadcasted_iota(jnp.int32, (rows, LANES), 1)
    for k in range(shards):
        shard = lanes_of(k, 0)[0]
        level = jnp.zeros((rows, LANES), F32)
        for x in range(heads_here):
            first = (k * heads_here + x) * rows
            result = wide[first : first + rows, lanes_of(k, x)[1]].astype(BF16)
            for copy in range(copies):
                out[shard * copies + copy, :, x * LANES : (x + 1) * LANES] = result
            level = jnp.where(at // 3 == x, column[first : first + rows, :], level)
        high, middle, low = thirds(level)
        kind = lax.rem(at, 3)
        level = jnp.where(kind == 0, high, jnp.where(kind == 1, middle, low)).astype(BF16)
        for copy in range(copies):
            out[shard * copies + copy, :, width : width + LANES] = level
    if out.shape[2] > width + LANES:
        piece = hidden.shape[1] // shards
        share = gain.shape[1] // copies
        first = pl.multiple_of(lax.axis_index("expert") * share, share)
        parts = thirds(gain[:, pl.ds(first, share)])
        of_row = lax.broadcasted_iota(jnp.int32, (rows, share), 0)
        lines = jnp.zeros((rows, share), F32)
        for i, part in enumerate(parts):
            lines = jnp.where(of_row == i, jnp.broadcast_to(part, lines.shape), lines)
        lines = lines.astype(BF16)
        for shard in range(shards):
            for copy in range(copies):
                here = shard * copies + copy
                out[here, :, width + LANES : width + LANES + piece] = hidden[
                    :, shard * piece : (shard + 1) * piece
                ]
                out[here, :, width + LANES + piece :] = lines


def attend(lengths, table, after, hidden, gain, queries, keys, values, copies, per_kv, extra):
    shards = len(queries)
    rows, width = queries[0].shape
    depth = keys.shape[2]
    total_rows = shards * width // LANES * rows
    return pl.pallas_call(
        functools.partial(attend_kernel, (copies, per_kv, shards)),
        name="attend",
        out_shape=jax.ShapeDtypeStruct((shards * copies, rows, width + LANES + extra), BF16),
        in_specs=[SMEM, SMEM, ANY] + [VMEM] * (shards + 4),
        out_specs=VMEM,
        scratch_shapes=[pltpu.VMEM((total_rows, depth), F32), pltpu.VMEM((total_rows, LANES), F32)],
        compiler_params=pltpu.CompilerParams(vmem_limit_bytes=16 * MIB),
    )(lengths, table, after, hidden, gain, *queries, keys, values)


def project_kernel(dims, after, received, weight, *refs):
    del after
    shards, per_column, piece, extra = dims
    rest, (out, out_full, gain_out, gathered, placed) = refs[:-5], refs[-5:]
    copies = received.shape[0] // shards
    rows = received.shape[1]
    width = received.shape[2] - LANES - extra
    for e in range(copies):
        levels, outputs = [], []
        for s in range(shards):
            block = received[s * copies + e].astype(F32)
            parts = block[:, width : width + LANES]
            levels.append(
                parts
                + pltpu.roll(parts, LANES - 1, 1)
                + pltpu.roll(parts, LANES - 2, 1)
            )
            outputs.append(block[:, :width])
        joint = functools.reduce(jnp.maximum, levels)
        factors = [jnp.exp(level - joint) for level in levels]
        total = functools.reduce(jnp.add, factors)
        factors = [factor / total for factor in factors]
        for x in range(width // LANES):
            span = slice(x * LANES, (x + 1) * LANES)
            value = functools.reduce(
                jnp.add,
                [
                    factor[:, 3 * x : 3 * x + 1] * output[:, span]
                    for factor, output in zip(factors, outputs)
                ],
            )
            gathered[e * rows : (e + 1) * rows, span] = value
    if rest:
        residual = rest[0][...].astype(F32)
        gain_out[...] = rest[1][...]
    else:
        placed[...] = jnp.zeros_like(placed)
        for j in range(per_column):
            shard = lax.axis_index("expert") * per_column + j
            first = lax.axis_index("seq") * piece + j * piece * shards
            lanes = pl.ds(pl.multiple_of(first, piece), piece)
            for e in range(copies):
                block = received[shard * copies + e, :, width + LANES :].astype(F32)
                placed[e * rows : (e + 1) * rows, lanes] = block[:, :piece]
                at = (j * copies + e) * (extra - piece)
                gain_out[:, at : at + extra - piece] = jnp.sum(
                    block[:3, piece:], axis=0, keepdims=True
                )
        residual = placed[...]
    attention = gathered[...].astype(BF16)
    result = jnp.dot(attention, weight[...], preferred_element_type=F32) + residual
    out_full[...] = result
    out[...] = result.astype(BF16)


def project(after, received, weight, rest, shards, per_column, piece, extra):
    columns = weight.shape[1]
    tokens = received.shape[0] // shards * received.shape[1]
    return pl.pallas_call(
        functools.partial(project_kernel, (shards, per_column, piece, extra)),
        name="project",
        out_shape=[
            jax.ShapeDtypeStruct((tokens, columns), BF16),
            jax.ShapeDtypeStruct((tokens, columns), F32),
            jax.ShapeDtypeStruct((1, columns), F32),
        ],
        in_specs=[ANY] + [VMEM] * (2 + len(rest)),
        out_specs=[VMEM] * 3,
        scratch_shapes=[
            pltpu.VMEM((tokens, weight.shape[0]), F32),
            pltpu.VMEM((tokens, columns), F32),
        ],
        compiler_params=pltpu.CompilerParams(vmem_limit_bytes=4 * MIB),
        cost_estimate=pl.CostEstimate(flops=LONG, bytes_accessed=0, transcendentals=0),
    )(after, received, weight, *rest)


def residual_kernel(gain, own, *refs):
    parts, out = refs[:-1], refs[-1]
    resid = own[...]
    for part in parts:
        resid = resid + part[...].astype(F32)
    columns = resid.shape[1]
    out[:, :columns] = (resid * gain[...]).astype(BF16)
    squares = jnp.sum(resid * resid, axis=1, keepdims=True)
    high, middle, low = thirds(jnp.broadcast_to(squares, (resid.shape[0], LANES)))
    at = lax.broadcasted_iota(jnp.int32, high.shape, 1)
    tail = jnp.where(at == 0, high, jnp.where(at == 1, middle, jnp.where(at == 2, low, 0.0)))
    out[:, columns:] = tail.astype(BF16)


def residual_block(gain, own, parts):
    tokens, columns = own.shape
    return pl.pallas_call(
        residual_kernel,
        name="residual_block",
        out_shape=jax.ShapeDtypeStruct((tokens, columns + LANES), BF16),
        in_specs=[VMEM] * (len(parts) + 2),
        out_specs=VMEM,
        compiler_params=pltpu.CompilerParams(vmem_limit_bytes=2 * MIB),
        cost_estimate=pl.CostEstimate(flops=LONG, bytes_accessed=0, transcendentals=0),
    )(gain, own, *parts)


def join_kernel(*refs):
    blocks, out = refs[:-1], refs[-1]
    groups = len(blocks)
    for k, block in enumerate(blocks):
        out[lax.rem(lax.axis_index("batch") - k + groups, groups)] = block[...]


def join(blocks):
    return pl.pallas_call(
        join_kernel,
        name="join",
        out_shape=jax.ShapeDtypeStruct((len(blocks),) + blocks[0].shape, BF16),
        in_specs=[VMEM] * len(blocks),
        out_specs=VMEM,
        compiler_params=pltpu.CompilerParams(vmem_limit_bytes=MIB),
        cost_estimate=pl.CostEstimate(flops=LONG, bytes_accessed=0, transcendentals=0),
    )(*blocks)


def expert_kernel(dims, *refs):
    seq, own, group = [lax.axis_index(name) for name in ("seq", "expert", "batch")]
    column_blocks, shards, rows = dims
    blocks = refs[:column_blocks]
    gain, gate, up, down, out, resid, result, kept = refs[column_blocks:]
    groups, tokens, columns = blocks[0].shape
    columns -= LANES
    features = column_blocks * columns
    width = features // shards
    first = seq * width
    squares = 0.0
    gate_part = up_part = None
    for k in range(column_blocks):
        block = lax.rem(own - k + column_blocks, column_blocks)
        both = jnp.concatenate([blocks[k][g] for g in range(groups)], axis=0)
        tail = both[:, columns:].astype(F32)
        squares = squares + tail[:, 0:1] + tail[:, 1:2] + tail[:, 2:3]
        x = both[:, :columns]

        @pl.when(first // columns == block)
        def _(x=x):
            kept[...] = x.astype(F32)

        rows_of = pl.ds(pl.multiple_of(block * columns, columns), columns)
        gate_term = jnp.dot(x, gate[rows_of, :], preferred_element_type=F32)
        up_term = jnp.dot(x, up[rows_of, :], preferred_element_type=F32)
        gate_part = gate_term if gate_part is None else gate_part + gate_term
        up_part = up_term if up_part is None else up_part + up_term
    scale = lax.rsqrt(squares / features + EPS)
    gate_part = gate_part * scale
    up_part = up_part * scale
    act = (gate_part / (1.0 + jnp.exp(-gate_part)) * up_part).astype(BF16)
    result[...] = jnp.dot(act, down[...], preferred_element_type=F32)
    for s in range(shards):
        for e in range(column_blocks):
            for g in range(groups):
                at = g * tokens + e * rows
                out[(s * column_blocks + e) * groups + g] = result[
                    at : at + rows, s * width : (s + 1) * width
                ].astype(BF16)
    lanes = pl.ds(pl.multiple_of(lax.rem(first, columns), width), width)
    for block in range(groups * column_blocks):

        @pl.when(group * column_blocks + own == block)
        def _(block=block):
            resid[...] = kept[block * rows : (block + 1) * rows, lanes] / gain[...]


def expert(blocks, gain, gate, up, down, shards, rows):
    column_blocks = len(blocks)
    groups, tokens, columns = blocks[0].shape
    columns -= LANES
    features = column_blocks * columns
    return pl.pallas_call(
        functools.partial(expert_kernel, (column_blocks, shards, rows)),
        name="expert",
        out_shape=[
            jax.ShapeDtypeStruct((column_blocks * groups * shards, rows, features // shards), BF16),
            jax.ShapeDtypeStruct((rows, features // shards), F32),
        ],
        in_specs=[VMEM] * (column_blocks + 4),
        out_specs=[VMEM, VMEM],
        scratch_shapes=[
            pltpu.VMEM((groups * tokens, features), F32),
            pltpu.VMEM((groups * tokens, columns), F32),
        ],
        compiler_params=pltpu.CompilerParams(vmem_limit_bytes=27 * MIB),
    )(*blocks, gain, gate, up, down)


def finish_kernel(dims, ids, routes, returned, resid, out):
    shards, experts, groups = dims
    rows = out.shape[0]
    at = lax.broadcasted_iota(jnp.int32, (rows, 1), 0)
    total = resid[...]
    for e in range(experts):
        factor = jnp.zeros((rows, 1), F32)
        for i in range(rows):
            share = 0.0
            for k in range(ids.shape[1]):
                share = share + jnp.where(ids[i, k] == e, routes[i, k], 0.0)
            factor = jnp.where(at == i, share, factor)
        term = None
        for s in range(shards):
            for g in range(groups):
                part = returned[(s * experts + e) * groups + g].astype(F32)
                term = part if term is None else term + part
        total = total + factor * term
    out[...] = total.astype(BF16)


def finish(ids, routes, returned, resid, dims):
    return pl.pallas_call(
        functools.partial(finish_kernel, dims),
        name="finish",
        out_shape=jax.ShapeDtypeStruct(resid.shape, BF16),
        in_specs=[SMEM, SMEM, VMEM, VMEM],
        out_specs=VMEM,
        compiler_params=pltpu.CompilerParams(vmem_limit_bytes=4 * MIB),
    )(ids, routes, returned, resid)


def per_device(
    hidden_state,
    queries,
    page_table,
    lengths,
    paged_keys,
    paged_values,
    out_weight,
    norm_gain,
    expert_ids,
    route_weights,
    expert_gate,
    expert_up,
    expert_down,
):
    shards = lax.axis_size("seq")
    experts = lax.axis_size("expert")
    groups = lax.axis_size("batch")
    rows = hidden_state.shape[0]
    columns = out_weight.shape[1]
    kv_heads = paged_keys.shape[3] // LANES
    per_kv = shards * queries.shape[1] // LANES // kv_heads
    own_gain = norm_gain[None, :]
    own_features = hidden_state.shape[1]
    per_column = columns // own_features

    piece, share = own_features // shards, own_features // experts
    rest = []
    if piece % LANES or share % LANES or rows < 3:
        piece = share = 0
        everything = lax.all_gather(hidden_state, "expert", axis=0, tiled=True)
        everything = lax.all_gather(everything, "seq", axis=1, tiled=True)
        first = lax.axis_index("expert") * columns
        block = lax.dynamic_slice_in_dim(everything, first, columns, 1)
        gains = lax.all_gather(norm_gain, "seq", axis=0, tiled=True)
        rest = [
            jnp.where(lax.axis_index("seq") == 0, block, 0),
            lax.dynamic_slice_in_dim(gains, first, columns, 0)[None, :],
        ]

    partials = attend(
        lengths,
        page_table,
        pause(queries),
        hidden_state,
        own_gain,
        shifts_over(queries, "seq"),
        paged_keys[0],
        paged_values[0],
        experts,
        per_kv,
        piece + share,
    )
    received = lax.all_to_all(
        partials, ("seq", "expert"), split_axis=0, concat_axis=0, tiled=True
    )
    projected, own, gain = project(
        pause(partials), received, out_weight, rest, shards, per_column, piece, piece + share
    )

    parts = shifts_over(projected, "seq")[1:]
    block = residual_block(gain, own, parts)
    block = join(shifts_over(block, "batch"))
    gate, up, down = expert_gate[0], expert_up[0], expert_down[0]

    blocks = shifts_over(block, "expert")
    outputs, resid = expert(blocks, own_gain, gate, up, down, shards, rows)
    returned = lax.all_to_all(
        outputs, ("seq", "expert", "batch"), split_axis=0, concat_axis=0, tiled=True
    )
    return finish(expert_ids, route_weights, returned, resid, (shards, experts, groups))


def solution(mesh):
    in_specs = (
        P(("batch", "expert"), "seq"),
        P(("batch", "expert"), "seq"),
        P(("batch", "expert"), "seq", None),
        P(("batch", "expert")),
        P(("batch", "expert"), "seq", None, None),
        P(("batch", "expert"), "seq", None, None),
        P("seq", "expert"),
        P("seq"),
        P(("batch", "expert"), None),
        P(("batch", "expert"), None),
        P("expert", None, ("seq", "batch")),
        P("expert", None, ("seq", "batch")),
        P("expert", ("seq", "batch"), None),
    )
    out_specs = P(("batch", "expert"), "seq")
    return jax.shard_map(
        per_device, mesh=mesh, in_specs=in_specs, out_specs=out_specs, check_vma=False
    )
```

```python
import functools
import math

import jax
import jax.numpy as jnp
from jax import lax
from jax.experimental import pallas as pl
from jax.experimental.pallas import tpu as pltpu
from jax.sharding import PartitionSpec as P

LANES = 128
EPS = 1e-05
MIB = 1 << 20
LONG = 6 * 10**9
F32 = jnp.float32
BF16 = jnp.bfloat16


VMEM = pl.BlockSpec(memory_space=pltpu.VMEM)
SMEM = pl.BlockSpec(memory_space=pltpu.SMEM)
ANY = pl.BlockSpec(memory_space=pl.ANY)
HBM = pl.BlockSpec(memory_space=pltpu.HBM)


def in_vmem(array):
    return pltpu.with_memory_space_constraint(array, pltpu.VMEM)


def in_hbm(array):
    return pltpu.with_memory_space_constraint(array, pltpu.HBM)


def thirds(value):
    high = value.astype(BF16).astype(F32)
    rest = value - high
    middle = rest.astype(BF16).astype(F32)
    return high, middle, rest - middle


def exchange(block, axis):
    count = lax.axis_size(axis)
    assert count & (count - 1) == 0
    return [block] + [
        lax.ppermute(block, axis, [(i, i ^ k) for i in range(count)]) for k in range(1, count)
    ]


def owner(axis, slot):
    return lax.bitwise_xor(lax.axis_index(axis), slot)


def pause_kernel(after, out):
    del after
    out[...] = jnp.zeros_like(out)


def pause(after):
    return pl.pallas_call(
        pause_kernel,
        name="pause",
        out_shape=jax.ShapeDtypeStruct((8, LANES), F32),
        in_specs=[ANY],
        out_specs=VMEM,
        compiler_params=pltpu.CompilerParams(vmem_limit_bytes=MIB),
        cost_estimate=pl.CostEstimate(flops=6000000000, bytes_accessed=0, transcendentals=0),
    )(after)


def attend_kernel(dims, lengths, table, after, hidden, *refs):
    del after
    copies, per_kv, shards = dims
    queries, (keys, values, _, out, wide, column) = refs[:shards], refs[shards:]
    rows, _, slots = table.shape
    heads_here = queries[0].shape[1] // LANES
    page = keys.shape[1]
    span = slots * page
    total_rows = wide.shape[0]
    own = lax.axis_index("seq")

    def lanes_of(k, x):
        shard = owner("seq", k)
        first = (shard * heads_here + x) // per_kv * LANES
        return shard, pl.ds(pl.multiple_of(first, LANES), LANES)

    wide[...] = jnp.zeros_like(wide)
    for k in range(shards):
        for x in range(heads_here):
            first = (k * heads_here + x) * rows
            wide[first : first + rows, lanes_of(k, x)[1]] = queries[k][
                :, x * LANES : (x + 1) * LANES
            ].astype(F32)
    spread = wide[...].astype(BF16)

    row_kind = lax.rem(lax.broadcasted_iota(jnp.int32, (total_rows, 1), 0), rows)
    length = jnp.zeros((total_rows, 1), jnp.int32)
    for i in range(rows):
        length = jnp.where(row_kind == i, lengths[i], length)
    lane = lax.broadcasted_iota(jnp.int32, (1, span), 1)
    position = (lane // page * shards + own) * page + lax.rem(lane, page)

    pages = []
    for j in range(slots):
        scores = jnp.zeros((total_rows, page), F32)
        for i in range(rows):
            part = lax.dot_general(
                spread,
                keys[table[i, 0, j]],
                (((1,), (1,)), ((), ())),
                preferred_element_type=F32,
            )
            scores = jnp.where(row_kind == i, part, scores)
        pages.append(scores)
    scores = jnp.concatenate(pages, axis=1)
    scores = jnp.where(position < length, scores / math.sqrt(LANES), -1e30)
    peak = jnp.max(scores, axis=1, keepdims=True)
    powers = jnp.exp(scores - peak)
    total = jnp.sum(powers, axis=1, keepdims=True)

    summed = jnp.zeros(wide.shape, F32)
    for i in range(rows):
        weights = jnp.where(row_kind == i, powers, 0.0).astype(BF16)
        for j in range(slots):
            summed = summed + jnp.dot(
                weights[:, j * page : (j + 1) * page],
                values[table[i, 0, j]],
                preferred_element_type=F32,
            )
    wide[...] = summed / total
    column[...] = jnp.broadcast_to(peak + jnp.log(total), column.shape)

    width = heads_here * LANES
    at = lax.broadcasted_iota(jnp.int32, (rows, LANES), 1)
    for k in range(shards):
        shard = lanes_of(k, 0)[0]
        level = jnp.zeros((rows, LANES), F32)
        for x in range(heads_here):
            first = (k * heads_here + x) * rows
            result = wide[first : first + rows, lanes_of(k, x)[1]].astype(BF16)
            for copy in range(copies):
                out[shard * copies + copy, :, x * LANES : (x + 1) * LANES] = result
            level = jnp.where(at // 3 == x, column[first : first + rows, :], level)
        high, middle, low = thirds(level)
        kind = lax.rem(at, 3)
        level = jnp.where(kind == 0, high, jnp.where(kind == 1, middle, low)).astype(BF16)
        for copy in range(copies):
            out[shard * copies + copy, :, width : width + LANES] = level
    if out.shape[2] > width + LANES:
        piece = hidden.shape[1] // shards
        for shard in range(shards):
            for copy in range(copies):
                out[shard * copies + copy, :, width + LANES :] = hidden[
                    :, shard * piece : (shard + 1) * piece
                ]


def attend(lengths, table, after, hidden, queries, keys, values, early, copies, per_kv, extra):
    shards = len(queries)
    rows, width = queries[0].shape
    depth = keys.shape[2]
    total_rows = shards * width // LANES * rows
    return pl.pallas_call(
        functools.partial(attend_kernel, (copies, per_kv, shards)),
        name="attend",
        out_shape=jax.ShapeDtypeStruct((shards * copies, rows, width + LANES + extra), BF16),
        in_specs=[SMEM, SMEM, ANY] + [VMEM] * (shards + 4),
        out_specs=VMEM,
        scratch_shapes=[pltpu.VMEM((total_rows, depth), F32), pltpu.VMEM((total_rows, LANES), F32)],
        compiler_params=pltpu.CompilerParams(vmem_limit_bytes=16 * MIB),
    )(lengths, table, after, hidden, *queries, keys, values, early)


def project_kernel(dims, received, weight, *refs):
    shards, piece = dims
    rest, (out, out_full, gathered, placed) = refs[:-4], refs[-4:]
    copies = received.shape[0] // shards
    rows = received.shape[1]
    width = received.shape[2] - LANES - piece
    for e in range(copies):
        levels, outputs = [], []
        for s in range(shards):
            block = received[s * copies + e].astype(F32)
            parts = block[:, width : width + LANES]
            levels.append(
                parts
                + pltpu.roll(parts, LANES - 1, 1)
                + pltpu.roll(parts, LANES - 2, 1)
            )
            outputs.append(block[:, :width])
        joint = functools.reduce(jnp.maximum, levels)
        factors = [jnp.exp(level - joint) for level in levels]
        total = functools.reduce(jnp.add, factors)
        factors = [factor / total for factor in factors]
        for x in range(width // LANES):
            span = slice(x * LANES, (x + 1) * LANES)
            value = functools.reduce(
                jnp.add,
                [
                    factor[:, 3 * x : 3 * x + 1] * output[:, span]
                    for factor, output in zip(factors, outputs)
                ],
            )
            gathered[e * rows : (e + 1) * rows, span] = value
    if piece:
        placed[...] = jnp.zeros_like(placed)
        lanes = pl.ds(pl.multiple_of(lax.axis_index("seq") * piece, piece), piece)
        for e in range(copies):
            placed[e * rows : (e + 1) * rows, lanes] = received[
                lax.axis_index("expert") * copies + e, :, width + LANES :
            ].astype(F32)
        residual = placed[...]
    else:
        residual = rest[0][...].astype(F32)
    attention = gathered[...].astype(BF16)
    result = jnp.dot(attention, weight[...], preferred_element_type=F32) + residual
    out_full[...] = result
    out[: result.shape[0], :] = result.astype(BF16)
    if piece:
        for i, part in enumerate(thirds(rest[0][...])):
            out[result.shape[0] + i : result.shape[0] + i + 1, :] = part.astype(BF16)


def project(received, weight, rest, shards, piece):
    columns = weight.shape[1]
    tokens = received.shape[0] // shards * received.shape[1]
    return pl.pallas_call(
        functools.partial(project_kernel, (shards, piece)),
        name="project",
        out_shape=[
            jax.ShapeDtypeStruct((tokens + (3 if piece else 0), columns), BF16),
            jax.ShapeDtypeStruct((tokens, columns), F32),
        ],
        in_specs=[VMEM] * (2 + len(rest)),
        out_specs=[VMEM] * 2,
        scratch_shapes=[
            pltpu.VMEM((tokens, weight.shape[0]), F32),
            pltpu.VMEM((tokens, columns), F32),
        ],
        compiler_params=pltpu.CompilerParams(vmem_limit_bytes=4 * MIB),
        cost_estimate=pl.CostEstimate(flops=LONG, bytes_accessed=0, transcendentals=0),
    )(received, weight, *rest)


def residual_kernel(after, gain, own, *refs):
    del after
    parts, out = refs[:-1], refs[-1]
    tokens, columns = own.shape
    resid = own[...]
    factor = gain[...]
    for k, part in enumerate(parts):
        block = part[...].astype(F32)
        resid = resid + block[:tokens]
        if part.shape[0] > tokens:
            shard = owner("seq", k + 1)
            here = jnp.sum(block[tokens:], axis=0, keepdims=True)
            factor = jnp.where(shard == lax.axis_index("expert"), here, factor)
    out[:, :columns] = (resid * factor).astype(BF16)
    squares = jnp.sum(resid * resid, axis=1, keepdims=True)
    high, middle, low = thirds(jnp.broadcast_to(squares, (tokens, LANES)))
    at = lax.broadcasted_iota(jnp.int32, high.shape, 1)
    tail = jnp.where(at == 0, high, jnp.where(at == 1, middle, jnp.where(at == 2, low, 0.0)))
    out[:, columns:] = tail.astype(BF16)


def residual_block(after, gain, own, parts):
    tokens, columns = own.shape
    return pl.pallas_call(
        residual_kernel,
        name="residual_block",
        out_shape=jax.ShapeDtypeStruct((tokens, columns + LANES), BF16),
        in_specs=[ANY] + [VMEM] * (len(parts) + 2),
        out_specs=VMEM,
        compiler_params=pltpu.CompilerParams(vmem_limit_bytes=2 * MIB),
        cost_estimate=pl.CostEstimate(flops=1000000000, bytes_accessed=0, transcendentals=0),
    )(after, gain, own, *parts)


def join_kernel(*refs):
    blocks, out = refs[:-1], refs[-1]
    for k, block in enumerate(blocks):
        out[owner("batch", k)] = block[...]


def join(blocks):
    return pl.pallas_call(
        join_kernel,
        name="join",
        out_shape=jax.ShapeDtypeStruct((len(blocks),) + blocks[0].shape, BF16),
        in_specs=[VMEM] * len(blocks),
        out_specs=VMEM,
        compiler_params=pltpu.CompilerParams(vmem_limit_bytes=MIB),
        cost_estimate=pl.CostEstimate(flops=1000000000, bytes_accessed=0, transcendentals=0),
    )(*blocks)


def enter_kernel(dims, tokens_in, gate, up, *refs):
    slot, early = dims
    before, (out, squares) = refs[early:-2], refs[-2:]
    groups, _, columns = tokens_in.shape
    columns -= LANES
    hidden = gate.shape[1]
    block = owner("expert", slot)
    both = jnp.concatenate([tokens_in[g] for g in range(groups)], axis=0)
    tail = both[:, columns:].astype(F32)
    square = tail[:, 0:1] + tail[:, 1:2] + tail[:, 2:3]
    x = both[:, :columns]
    rows_of = pl.ds(pl.multiple_of(block * columns, columns), columns)
    gate_term = jnp.dot(x, gate[rows_of, :], preferred_element_type=F32)
    up_term = jnp.dot(x, up[rows_of, :], preferred_element_type=F32)
    if before:
        gate_term = gate_term + before[0][:, :hidden]
        up_term = up_term + before[0][:, hidden:]
        square = square + before[1][:, :1]
    out[:, :hidden] = gate_term
    out[:, hidden:] = up_term
    squares[...] = jnp.broadcast_to(square, squares.shape)


def enter(block, gate, up, early, before, slot):
    weights = [gate, up, *early] if early else [in_vmem(gate), in_vmem(up)]
    tokens = block.shape[0] * block.shape[1]
    return pl.pallas_call(
        functools.partial(enter_kernel, (slot, len(early))),
        name="enter",
        out_shape=[
            jax.ShapeDtypeStruct((tokens, 2 * gate.shape[1]), F32),
            jax.ShapeDtypeStruct((tokens, LANES), F32),
        ],
        in_specs=[VMEM] * (3 + len(early) + len(before)),
        out_specs=[VMEM] * 2,
        compiler_params=pltpu.CompilerParams(vmem_limit_bytes=(26 if early else 6) * MIB),
        cost_estimate=pl.CostEstimate(flops=1000000, bytes_accessed=0, transcendentals=0),
    )(block, *weights, *before)


def leave_kernel(dims, entered, squares, gain, down, ids, routes, *refs):
    shards, rows = dims
    blocks, (out, resid, mix, result, kept) = refs[:-5], refs[-5:]
    choices, count = ids.shape
    line = lax.broadcasted_iota(jnp.int32, (count, count), 0)
    same = line == lax.broadcasted_iota(jnp.int32, (count, count), 1)
    at = lax.broadcasted_iota(jnp.int32, mix.shape, 1)
    shares = jnp.zeros(mix.shape, F32)
    for k in range(choices):
        name = jnp.sum(jnp.where(same, ids[k : k + 1, :], 0), axis=1, keepdims=True)
        share = jnp.sum(jnp.where(same, routes[k : k + 1, :], 0.0), axis=1, keepdims=True)
        shares = shares + jnp.where(at == name, share, 0.0)
    mix[...] = shares
    seq, own, group = [lax.axis_index(name) for name in ("seq", "expert", "batch")]
    column_blocks = len(blocks)
    groups, tokens, columns = blocks[0].shape
    columns -= LANES
    features = column_blocks * columns
    width = features // shards
    hidden = down.shape[0]
    scale = lax.rsqrt(squares[:, :1] / features + EPS)
    gate_part = entered[:, :hidden] * scale
    up_part = entered[:, hidden:] * scale
    act = (gate_part / (1.0 + jnp.exp(-gate_part)) * up_part).astype(BF16)
    result[...] = jnp.dot(act, down[...], preferred_element_type=F32)
    for s in range(shards):
        for e in range(column_blocks):
            for g in range(groups):
                at = g * tokens + e * rows
                out[(s * column_blocks + e) * groups + g] = result[
                    at : at + rows, s * width : (s + 1) * width
                ].astype(BF16)
    first = seq * width
    lanes = pl.ds(pl.multiple_of(lax.rem(first, columns), width), width)
    for k in range(column_blocks):

        @pl.when(first // columns == owner("expert", k))
        def _(k=k):
            kept[...] = blocks[k][group].astype(F32)

    for e in range(column_blocks):

        @pl.when(own == e)
        def _(e=e):
            resid[...] = kept[e * rows : (e + 1) * rows, lanes] / gain[...]


def leave(entered, squares, gain, down, ids, routes, blocks, shards, rows):
    column_blocks = len(blocks)
    groups, tokens, columns = blocks[0].shape
    features = down.shape[1]
    return pl.pallas_call(
        functools.partial(leave_kernel, (shards, rows)),
        name="leave",
        out_shape=[
            jax.ShapeDtypeStruct((column_blocks * groups * shards, rows, features // shards), BF16),
            jax.ShapeDtypeStruct((rows, features // shards), F32),
            jax.ShapeDtypeStruct((rows, LANES), F32),
        ],
        in_specs=[VMEM] * (column_blocks + 6),
        out_specs=[VMEM] * 3,
        scratch_shapes=[
            pltpu.VMEM((groups * tokens, features), F32),
            pltpu.VMEM((tokens, columns), F32),
        ],
        compiler_params=pltpu.CompilerParams(vmem_limit_bytes=11 * MIB),
    )(entered, squares, gain, down, ids, routes, *blocks)


def finish_kernel(dims, mix, returned, resid, out):
    shards, experts, groups = dims
    total = resid[...]
    for e in range(experts):
        term = None
        for s in range(shards):
            for g in range(groups):
                part = returned[(s * experts + e) * groups + g].astype(F32)
                term = part if term is None else term + part
        total = total + mix[:, e : e + 1] * term
    out[...] = total.astype(BF16)


def finish(mix, returned, resid, dims):
    return pl.pallas_call(
        functools.partial(finish_kernel, dims),
        name="finish",
        out_shape=jax.ShapeDtypeStruct(resid.shape, BF16),
        in_specs=[VMEM] * 3,
        out_specs=VMEM,
        compiler_params=pltpu.CompilerParams(vmem_limit_bytes=4 * MIB),
    )(mix, returned, resid)


def per_device(
    hidden_state,
    queries,
    page_table,
    lengths,
    paged_keys,
    paged_values,
    out_weight,
    norm_gain,
    expert_ids,
    route_weights,
    expert_gate,
    expert_up,
    expert_down,
):
    shards = lax.axis_size("seq")
    experts = lax.axis_size("expert")
    groups = lax.axis_size("batch")
    rows = hidden_state.shape[0]
    columns = out_weight.shape[1]
    kv_heads = paged_keys.shape[3] // LANES
    per_kv = shards * queries.shape[1] // LANES // kv_heads
    own_gain = norm_gain[None, :]
    own_features = hidden_state.shape[1]

    piece = own_features // shards
    if own_features == columns and piece % LANES == 0:
        rest = [own_gain]
        gain = own_gain
    else:
        piece = 0
        everything = lax.all_gather(hidden_state, "expert", axis=0, tiled=True)
        everything = lax.all_gather(everything, "seq", axis=1, tiled=True)
        first = lax.axis_index("expert") * columns
        block = lax.dynamic_slice_in_dim(everything, first, columns, 1)
        gain = lax.all_gather(norm_gain, "seq", axis=0, tiled=True)
        gain = lax.dynamic_slice_in_dim(gain, first, columns, 0)[None, :]
        rest = [jnp.where(lax.axis_index("seq") == 0, block, 0)]

    partials = attend(
        lengths,
        page_table,
        pause(in_hbm(queries)),
        hidden_state,
        exchange(queries, "seq"),
        paged_keys[0],
        paged_values[0],
        out_weight,
        experts,
        per_kv,
        piece,
    )
    received = lax.all_to_all(
        partials, ("seq", "expert"), split_axis=0, concat_axis=0, tiled=True
    )
    projected, own = project(received, out_weight, rest, shards, piece)

    parts = exchange(projected, "seq")[1:]
    block = residual_block(pause(projected), gain, own, parts)
    block = join(exchange(block, "batch"))
    gate, up, down = expert_gate[0], expert_up[0], expert_down[0]

    blocks = exchange(block, "expert")
    entered = []
    for slot, block in enumerate(blocks):
        early = [] if slot else [down]
        entered = enter(block, gate, up, early, entered, slot)
    outputs, resid, mix = leave(
        *entered, own_gain, down, expert_ids.T, route_weights.T, blocks, shards, rows
    )
    returned = lax.all_to_all(
        outputs, ("seq", "expert", "batch"), split_axis=0, concat_axis=0, tiled=True
    )
    return finish(mix, returned, resid, (shards, experts, groups))


def solution(mesh):
    in_specs = (
        P(("batch", "expert"), "seq"),
        P(("batch", "expert"), "seq"),
        P(("batch", "expert"), "seq", None),
        P(("batch", "expert")),
        P(("batch", "expert"), "seq", None, None),
        P(("batch", "expert"), "seq", None, None),
        P("seq", "expert"),
        P("seq"),
        P(("batch", "expert"), None),
        P(("batch", "expert"), None),
        P("expert", None, ("seq", "batch")),
        P("expert", None, ("seq", "batch")),
        P("expert", ("seq", "batch"), None),
    )
    out_specs = P(("batch", "expert"), "seq")
    return jax.shard_map(
        per_device, mesh=mesh, in_specs=in_specs, out_specs=out_specs, check_vma=False
    )
```

```python
import functools
import math

import jax
import jax.numpy as jnp
from jax import lax
from jax.experimental import pallas as pl
from jax.experimental.pallas import tpu as pltpu
from jax.sharding import PartitionSpec as P

LANES = 128
EPS = 1e-05
MIB = 1 << 20
LONG = 6 * 10**9
F32 = jnp.float32
BF16 = jnp.bfloat16


VMEM = pl.BlockSpec(memory_space=pltpu.VMEM)
SMEM = pl.BlockSpec(memory_space=pltpu.SMEM)
ANY = pl.BlockSpec(memory_space=pl.ANY)
HBM = pl.BlockSpec(memory_space=pltpu.HBM)


def in_vmem(array):
    return pltpu.with_memory_space_constraint(array, pltpu.VMEM)


def in_hbm(array):
    return pltpu.with_memory_space_constraint(array, pltpu.HBM)


def thirds(value):
    high = value.astype(BF16).astype(F32)
    rest = value - high
    middle = rest.astype(BF16).astype(F32)
    return high, middle, rest - middle


def exchange(block, axis):
    count = lax.axis_size(axis)
    assert count & (count - 1) == 0
    return [block] + [
        lax.ppermute(block, axis, [(i, i ^ k) for i in range(count)]) for k in range(1, count)
    ]


def owner(axis, slot):
    return lax.bitwise_xor(lax.axis_index(axis), slot)


def pause_kernel(after, out):
    del after
    out[...] = jnp.zeros_like(out)


def pause(after):
    return pl.pallas_call(
        pause_kernel,
        name="pause",
        out_shape=jax.ShapeDtypeStruct((8, LANES), F32),
        in_specs=[ANY],
        out_specs=VMEM,
        compiler_params=pltpu.CompilerParams(vmem_limit_bytes=MIB),
        cost_estimate=pl.CostEstimate(flops=6000000000, bytes_accessed=0, transcendentals=0),
    )(after)


def attend_kernel(dims, lengths, table, after, hidden, *refs):
    del after
    copies, per_kv, shards = dims
    queries, (keys, values, _, out, wide, column) = refs[:shards], refs[shards:]
    rows, _, slots = table.shape
    heads_here = queries[0].shape[1] // LANES
    page = keys.shape[1]
    span = slots * page
    total_rows = wide.shape[0]
    own = lax.axis_index("seq")

    def lanes_of(k, x):
        shard = owner("seq", k)
        first = (shard * heads_here + x) // per_kv * LANES
        return shard, pl.ds(pl.multiple_of(first, LANES), LANES)

    wide[...] = jnp.zeros_like(wide)
    for k in range(shards):
        for x in range(heads_here):
            first = (k * heads_here + x) * rows
            wide[first : first + rows, lanes_of(k, x)[1]] = queries[k][
                :, x * LANES : (x + 1) * LANES
            ].astype(F32)
    spread = wide[...].astype(BF16)

    row_kind = lax.rem(lax.broadcasted_iota(jnp.int32, (total_rows, 1), 0), rows)
    length = jnp.zeros((total_rows, 1), jnp.int32)
    for i in range(rows):
        length = jnp.where(row_kind == i, lengths[i], length)
    lane = lax.broadcasted_iota(jnp.int32, (1, span), 1)
    position = (lane // page * shards + own) * page + lax.rem(lane, page)

    pages = []
    for j in range(slots):
        scores = jnp.zeros((total_rows, page), F32)
        for i in range(rows):
            part = lax.dot_general(
                spread,
                keys[table[i, 0, j]],
                (((1,), (1,)), ((), ())),
                preferred_element_type=F32,
            )
            scores = jnp.where(row_kind == i, part, scores)
        pages.append(scores)
    scores = jnp.concatenate(pages, axis=1)
    scores = jnp.where(position < length, scores / math.sqrt(LANES), -1e30)
    peak = jnp.max(scores, axis=1, keepdims=True)
    powers = jnp.exp(scores - peak)
    total = jnp.sum(powers, axis=1, keepdims=True)

    summed = jnp.zeros(wide.shape, F32)
    for i in range(rows):
        weights = jnp.where(row_kind == i, powers, 0.0).astype(BF16)
        for j in range(slots):
            summed = summed + jnp.dot(
                weights[:, j * page : (j + 1) * page],
                values[table[i, 0, j]],
                preferred_element_type=F32,
            )
    wide[...] = summed / total
    column[...] = jnp.broadcast_to(peak + jnp.log(total), column.shape)

    width = heads_here * LANES
    at = lax.broadcasted_iota(jnp.int32, (rows, LANES), 1)
    for k in range(shards):
        shard = lanes_of(k, 0)[0]
        level = jnp.zeros((rows, LANES), F32)
        for x in range(heads_here):
            first = (k * heads_here + x) * rows
            result = wide[first : first + rows, lanes_of(k, x)[1]].astype(BF16)
            for copy in range(copies):
                out[shard * copies + copy, :, x * LANES : (x + 1) * LANES] = result
            level = jnp.where(at // 3 == x, column[first : first + rows, :], level)
        high, middle, low = thirds(level)
        kind = lax.rem(at, 3)
        level = jnp.where(kind == 0, high, jnp.where(kind == 1, middle, low)).astype(BF16)
        for copy in range(copies):
            out[shard * copies + copy, :, width : width + LANES] = level
    if out.shape[2] > width + LANES:
        piece = hidden.shape[1] // shards
        for shard in range(shards):
            for copy in range(copies):
                out[shard * copies + copy, :, width + LANES :] = hidden[
                    :, shard * piece : (shard + 1) * piece
                ]


def attend(lengths, table, after, hidden, queries, keys, values, early, copies, per_kv, extra):
    shards = len(queries)
    rows, width = queries[0].shape
    depth = keys.shape[2]
    total_rows = shards * width // LANES * rows
    return pl.pallas_call(
        functools.partial(attend_kernel, (copies, per_kv, shards)),
        name="attend",
        out_shape=jax.ShapeDtypeStruct((shards * copies, rows, width + LANES + extra), BF16),
        in_specs=[SMEM, SMEM, ANY] + [VMEM] * (shards + 4),
        out_specs=VMEM,
        scratch_shapes=[pltpu.VMEM((total_rows, depth), F32), pltpu.VMEM((total_rows, LANES), F32)],
        compiler_params=pltpu.CompilerParams(vmem_limit_bytes=16 * MIB),
    )(lengths, table, after, hidden, *queries, keys, values, early)


def project_kernel(dims, received, weight, *refs):
    shards, piece = dims
    rest, (out, out_full, gathered, placed) = refs[:-4], refs[-4:]
    copies = received.shape[0] // shards
    rows = received.shape[1]
    width = received.shape[2] - LANES - piece
    for e in range(copies):
        levels, outputs = [], []
        for s in range(shards):
            block = received[s * copies + e].astype(F32)
            parts = block[:, width : width + LANES]
            levels.append(
                parts
                + pltpu.roll(parts, LANES - 1, 1)
                + pltpu.roll(parts, LANES - 2, 1)
            )
            outputs.append(block[:, :width])
        joint = functools.reduce(jnp.maximum, levels)
        factors = [jnp.exp(level - joint) for level in levels]
        total = functools.reduce(jnp.add, factors)
        factors = [factor / total for factor in factors]
        for x in range(width // LANES):
            span = slice(x * LANES, (x + 1) * LANES)
            value = functools.reduce(
                jnp.add,
                [
                    factor[:, 3 * x : 3 * x + 1] * output[:, span]
                    for factor, output in zip(factors, outputs)
                ],
            )
            gathered[e * rows : (e + 1) * rows, span] = value
    if piece:
        placed[...] = jnp.zeros_like(placed)
        lanes = pl.ds(pl.multiple_of(lax.axis_index("seq") * piece, piece), piece)
        for e in range(copies):
            placed[e * rows : (e + 1) * rows, lanes] = received[
                lax.axis_index("expert") * copies + e, :, width + LANES :
            ].astype(F32)
        residual = placed[...]
    else:
        residual = rest[0][...].astype(F32)
    attention = gathered[...].astype(BF16)
    result = jnp.dot(attention, weight[...], preferred_element_type=F32) + residual
    out_full[...] = result
    out[:, : result.shape[1]] = result.astype(BF16)
    if piece:
        tokens, columns = result.shape
        lanes = 2 * columns // tokens
        for i, part in enumerate(thirds(rest[0][...])[:2]):
            for r in range(tokens // 2):
                at = i * tokens // 2 + r
                out[at : at + 1, columns:] = part[:, r * lanes : (r + 1) * lanes].astype(BF16)


def project(received, weight, rest, shards, piece):
    columns = weight.shape[1]
    tokens = received.shape[0] // shards * received.shape[1]
    return pl.pallas_call(
        functools.partial(project_kernel, (shards, piece)),
        name="project",
        out_shape=[
            jax.ShapeDtypeStruct(
                (tokens, columns + (2 * columns // tokens if piece else 0)), BF16
            ),
            jax.ShapeDtypeStruct((tokens, columns), F32),
        ],
        in_specs=[VMEM] * (2 + len(rest)),
        out_specs=[VMEM] * 2,
        scratch_shapes=[
            pltpu.VMEM((tokens, weight.shape[0]), F32),
            pltpu.VMEM((tokens, columns), F32),
        ],
        compiler_params=pltpu.CompilerParams(vmem_limit_bytes=4 * MIB),
        cost_estimate=pl.CostEstimate(flops=LONG, bytes_accessed=0, transcendentals=0),
    )(received, weight, *rest)


def residual_kernel(after, gain, own, *refs):
    del after
    parts, (out, gains) = refs[:-2], refs[-2:]
    tokens, columns = own.shape
    resid = own[...]
    if gain.shape[0] == gains.shape[0]:
        gains[...] = gain[...]
    else:
        gains[owner("seq", 0)] = gain[0]
    for k, part in enumerate(parts):
        block = part[...].astype(F32)
        resid = resid + block[:, :columns]
        if part.shape[1] > columns:
            both = block[: tokens // 2, columns:] + block[tokens // 2 :, columns:]
            gains[owner("seq", k + 1)] = jnp.concatenate(
                [both[r : r + 1] for r in range(tokens // 2)], axis=1
            )
    out[...] = (resid * gains[lax.axis_index("expert")]).astype(BF16)


def residual_block(after, gain, own, parts, column_blocks):
    tokens, columns = own.shape
    return pl.pallas_call(
        residual_kernel,
        name="residual_block",
        out_shape=[
            jax.ShapeDtypeStruct((tokens, columns), BF16),
            jax.ShapeDtypeStruct((column_blocks, 1, columns), F32),
        ],
        in_specs=[ANY] + [VMEM] * (len(parts) + 2),
        out_specs=[VMEM] * 2,
        compiler_params=pltpu.CompilerParams(vmem_limit_bytes=2 * MIB),
        cost_estimate=pl.CostEstimate(flops=1000000000, bytes_accessed=0, transcendentals=0),
    )(after, gain, own, *parts)


def join_kernel(*refs):
    blocks, out = refs[:-1], refs[-1]
    for k, block in enumerate(blocks):
        out[owner("batch", k)] = block[...]


def join(blocks):
    return pl.pallas_call(
        join_kernel,
        name="join",
        out_shape=jax.ShapeDtypeStruct((len(blocks),) + blocks[0].shape, BF16),
        in_specs=[VMEM] * len(blocks),
        out_specs=VMEM,
        compiler_params=pltpu.CompilerParams(vmem_limit_bytes=MIB),
        cost_estimate=pl.CostEstimate(flops=1000000000, bytes_accessed=0, transcendentals=0),
    )(*blocks)


def enter_kernel(dims, gains, tokens_in, gate, up, *refs):
    slot, early = dims
    before, (out, squares) = refs[early:-2], refs[-2:]
    groups, _, columns = tokens_in.shape
    hidden = gate.shape[1]
    block = owner("expert", slot)
    x = jnp.concatenate([tokens_in[g] for g in range(groups)], axis=0)
    plain = x.astype(F32) * (1.0 / gains[block])
    square = jnp.sum(plain * plain, axis=1, keepdims=True)
    rows_of = pl.ds(pl.multiple_of(block * columns, columns), columns)
    gate_term = jnp.dot(x, gate[rows_of, :], preferred_element_type=F32)
    up_term = jnp.dot(x, up[rows_of, :], preferred_element_type=F32)
    if before:
        gate_term = gate_term + before[0][:, :hidden]
        up_term = up_term + before[0][:, hidden:]
        square = square + before[1][:, :1]
    out[:, :hidden] = gate_term
    out[:, hidden:] = up_term
    squares[...] = jnp.broadcast_to(square, squares.shape)


def enter(gains, block, gate, up, early, before, slot):
    weights = [gate, up, *early] if early else [in_vmem(gate), in_vmem(up)]
    tokens = block.shape[0] * block.shape[1]
    return pl.pallas_call(
        functools.partial(enter_kernel, (slot, len(early))),
        name="enter",
        out_shape=[
            jax.ShapeDtypeStruct((tokens, 2 * gate.shape[1]), F32),
            jax.ShapeDtypeStruct((tokens, LANES), F32),
        ],
        in_specs=[VMEM] * (4 + len(early) + len(before)),
        out_specs=[VMEM] * 2,
        compiler_params=pltpu.CompilerParams(vmem_limit_bytes=(26 if early else 6) * MIB),
        cost_estimate=pl.CostEstimate(flops=1000000, bytes_accessed=0, transcendentals=0),
    )(gains, block, *weights, *before)


def leave_kernel(dims, entered, squares, gain, down, ids, routes, *refs):
    shards, rows = dims
    blocks, (out, resid, mix, result, kept) = refs[:-5], refs[-5:]
    choices, count = ids.shape
    line = lax.broadcasted_iota(jnp.int32, (count, count), 0)
    same = line == lax.broadcasted_iota(jnp.int32, (count, count), 1)
    at = lax.broadcasted_iota(jnp.int32, mix.shape, 1)
    shares = jnp.zeros(mix.shape, F32)
    for k in range(choices):
        name = jnp.sum(jnp.where(same, ids[k : k + 1, :], 0), axis=1, keepdims=True)
        share = jnp.sum(jnp.where(same, routes[k : k + 1, :], 0.0), axis=1, keepdims=True)
        shares = shares + jnp.where(at == name, share, 0.0)
    mix[...] = shares
    seq, own, group = [lax.axis_index(name) for name in ("seq", "expert", "batch")]
    column_blocks = len(blocks)
    groups, tokens, columns = blocks[0].shape
    features = column_blocks * columns
    width = features // shards
    hidden = down.shape[0]
    scale = lax.rsqrt(squares[:, :1] / features + EPS)
    gate_part = entered[:, :hidden] * scale
    up_part = entered[:, hidden:] * scale
    act = (gate_part / (1.0 + jnp.exp(-gate_part)) * up_part).astype(BF16)
    result[...] = jnp.dot(act, down[...], preferred_element_type=F32)
    for s in range(shards):
        for e in range(column_blocks):
            for g in range(groups):
                at = g * tokens + e * rows
                out[(s * column_blocks + e) * groups + g] = result[
                    at : at + rows, s * width : (s + 1) * width
                ].astype(BF16)
    first = seq * width
    lanes = pl.ds(pl.multiple_of(lax.rem(first, columns), width), width)
    for k in range(column_blocks):

        @pl.when(first // columns == owner("expert", k))
        def _(k=k):
            kept[...] = blocks[k][group].astype(F32)

    for e in range(column_blocks):

        @pl.when(own == e)
        def _(e=e):
            resid[...] = kept[e * rows : (e + 1) * rows, lanes] / gain[...]


def leave(entered, squares, gain, down, ids, routes, blocks, shards, rows):
    column_blocks = len(blocks)
    groups, tokens, columns = blocks[0].shape
    features = down.shape[1]
    return pl.pallas_call(
        functools.partial(leave_kernel, (shards, rows)),
        name="leave",
        out_shape=[
            jax.ShapeDtypeStruct((column_blocks * groups * shards, rows, features // shards), BF16),
            jax.ShapeDtypeStruct((rows, features // shards), F32),
            jax.ShapeDtypeStruct((rows, LANES), F32),
        ],
        in_specs=[VMEM] * (column_blocks + 6),
        out_specs=[VMEM] * 3,
        scratch_shapes=[
            pltpu.VMEM((groups * tokens, features), F32),
            pltpu.VMEM((tokens, columns), F32),
        ],
        compiler_params=pltpu.CompilerParams(vmem_limit_bytes=11 * MIB),
    )(entered, squares, gain, down, ids, routes, *blocks)


def finish_kernel(dims, mix, returned, resid, out):
    shards, experts, groups = dims
    total = resid[...]
    for e in range(experts):
        term = None
        for s in range(shards):
            for g in range(groups):
                part = returned[(s * experts + e) * groups + g].astype(F32)
                term = part if term is None else term + part
        total = total + mix[:, e : e + 1] * term
    out[...] = total.astype(BF16)


def finish(mix, returned, resid, dims):
    return pl.pallas_call(
        functools.partial(finish_kernel, dims),
        name="finish",
        out_shape=jax.ShapeDtypeStruct(resid.shape, BF16),
        in_specs=[VMEM] * 3,
        out_specs=VMEM,
        compiler_params=pltpu.CompilerParams(vmem_limit_bytes=4 * MIB),
    )(mix, returned, resid)


def per_device(
    hidden_state,
    queries,
    page_table,
    lengths,
    paged_keys,
    paged_values,
    out_weight,
    norm_gain,
    expert_ids,
    route_weights,
    expert_gate,
    expert_up,
    expert_down,
):
    shards = lax.axis_size("seq")
    experts = lax.axis_size("expert")
    groups = lax.axis_size("batch")
    rows = hidden_state.shape[0]
    columns = out_weight.shape[1]
    kv_heads = paged_keys.shape[3] // LANES
    per_kv = shards * queries.shape[1] // LANES // kv_heads
    own_gain = norm_gain[None, :]
    own_features = hidden_state.shape[1]

    piece = own_features // shards
    if own_features == columns and piece % LANES == 2 * columns % (experts * rows * LANES) == 0:
        rest = [own_gain]
        gain = own_gain[None]
    else:
        piece = 0
        everything = lax.all_gather(hidden_state, "expert", axis=0, tiled=True)
        everything = lax.all_gather(everything, "seq", axis=1, tiled=True)
        first = lax.axis_index("expert") * columns
        block = lax.dynamic_slice_in_dim(everything, first, columns, 1)
        gain = lax.all_gather(norm_gain, "seq", axis=0, tiled=True)
        gain = gain.reshape(experts, 1, columns)
        rest = [jnp.where(lax.axis_index("seq") == 0, block, 0)]

    partials = attend(
        lengths,
        page_table,
        pause(in_hbm(queries)),
        hidden_state,
        exchange(queries, "seq"),
        paged_keys[0],
        paged_values[0],
        out_weight,
        experts,
        per_kv,
        piece,
    )
    received = lax.all_to_all(
        partials, ("seq", "expert"), split_axis=0, concat_axis=0, tiled=True
    )
    projected, own = project(received, out_weight, rest, shards, piece)

    parts = exchange(projected, "seq")[1:]
    block, gains = residual_block(pause(projected), gain, own, parts, experts)
    block = join(exchange(block, "batch"))
    gate, up, down = expert_gate[0], expert_up[0], expert_down[0]

    blocks = exchange(block, "expert")
    entered = []
    for slot, block in enumerate(blocks):
        early = [] if slot else [down]
        entered = enter(gains, block, gate, up, early, entered, slot)
    outputs, resid, mix = leave(
        *entered, own_gain, down, expert_ids.T, route_weights.T, blocks, shards, rows
    )
    returned = lax.all_to_all(
        outputs, ("seq", "expert", "batch"), split_axis=0, concat_axis=0, tiled=True
    )
    return finish(mix, returned, resid, (shards, experts, groups))


def solution(mesh):
    in_specs = (
        P(("batch", "expert"), "seq"),
        P(("batch", "expert"), "seq"),
        P(("batch", "expert"), "seq", None),
        P(("batch", "expert")),
        P(("batch", "expert"), "seq", None, None),
        P(("batch", "expert"), "seq", None, None),
        P("seq", "expert"),
        P("seq"),
        P(("batch", "expert"), None),
        P(("batch", "expert"), None),
        P("expert", None, ("seq", "batch")),
        P("expert", None, ("seq", "batch")),
        P("expert", ("seq", "batch"), None),
    )
    out_specs = P(("batch", "expert"), "seq")
    return jax.shard_map(
        per_device, mesh=mesh, in_specs=in_specs, out_specs=out_specs, check_vma=False
    )
```

```python
import functools
import math

import jax
import jax.numpy as jnp
from jax import lax
from jax.experimental import pallas as pl
from jax.experimental.pallas import tpu as pltpu
from jax.sharding import PartitionSpec as P

LANES = 128
EPS = 1e-05
MIB = 1 << 20
LONG = 6 * 10**9
F32 = jnp.float32
BF16 = jnp.bfloat16


VMEM = pl.BlockSpec(memory_space=pltpu.VMEM)
SMEM = pl.BlockSpec(memory_space=pltpu.SMEM)
ANY = pl.BlockSpec(memory_space=pl.ANY)
HBM = pl.BlockSpec(memory_space=pltpu.HBM)


def in_vmem(array):
    return pltpu.with_memory_space_constraint(array, pltpu.VMEM)


def in_hbm(array):
    return pltpu.with_memory_space_constraint(array, pltpu.HBM)


def thirds(value):
    high = value.astype(BF16).astype(F32)
    rest = value - high
    middle = rest.astype(BF16).astype(F32)
    return high, middle, rest - middle


def exchange(block, axis):
    count = lax.axis_size(axis)
    assert count & (count - 1) == 0
    return [block] + [
        lax.ppermute(block, axis, [(i, i ^ k) for i in range(count)]) for k in range(1, count)
    ]


def owner(axis, slot):
    return lax.bitwise_xor(lax.axis_index(axis), slot)


def pause_kernel(after, out):
    del after
    out[...] = jnp.zeros_like(out)


def pause(after):
    return pl.pallas_call(
        pause_kernel,
        name="pause",
        out_shape=jax.ShapeDtypeStruct((8, LANES), F32),
        in_specs=[ANY],
        out_specs=VMEM,
        compiler_params=pltpu.CompilerParams(vmem_limit_bytes=MIB),
        cost_estimate=pl.CostEstimate(flops=6000000000, bytes_accessed=0, transcendentals=0),
    )(after)


def attend_kernel(dims, lengths, table, after, hidden, *refs):
    del after
    copies, per_kv, shards = dims
    queries, (keys, values, _, out, wide, column) = refs[:shards], refs[shards:]
    rows, _, slots = table.shape
    heads_here = queries[0].shape[1] // LANES
    page = keys.shape[1]
    span = slots * page
    own = lax.axis_index("seq")

    heads = shards * heads_here
    kinds = keys.shape[2] // LANES
    line = lax.broadcasted_iota(jnp.int32, (heads, 1), 0)
    kind = jnp.zeros((heads, 1), jnp.int32)
    for k in range(shards):
        head = owner("seq", k) * heads_here + lax.rem(line, heads_here)
        kind = jnp.where(line // heads_here == k, head // per_kv, kind)
        for x in range(heads_here):
            wide[pl.ds(k * heads_here + x, rows, stride=heads), :] = queries[k][
                :, x * LANES : (x + 1) * LANES
            ].astype(F32)

    lane = lax.broadcasted_iota(jnp.int32, (1, span), 1)
    position = (lane // page * shards + own) * page + lax.rem(lane, page)
    lines = [slice(i * heads, (i + 1) * heads) for i in range(rows)]
    every = jnp.concatenate([kind] * rows, axis=0)
    asked = wide[...]
    spread = jnp.concatenate(
        [jnp.where(every == v, asked, 0.0) for v in range(kinds)], axis=1
    ).astype(BF16)
    scores = jnp.concatenate(
        [
            jnp.concatenate(
                [
                    lax.dot_general(
                        spread[lines[i]],
                        keys[table[i, 0, j]],
                        (((1,), (1,)), ((), ())),
                        preferred_element_type=F32,
                    )
                    for j in range(slots)
                ],
                axis=1,
            )
            for i in range(rows)
        ],
        axis=0,
    )
    sequence = lax.broadcasted_iota(jnp.int32, (rows * heads, 1), 0) // heads
    length = jnp.zeros((rows * heads, 1), jnp.int32)
    for i in range(rows):
        length = jnp.where(sequence == i, lengths[i], length)
    scores = jnp.where(position < length, scores / math.sqrt(LANES), -1e30)
    peak = jnp.max(scores, axis=1, keepdims=True)
    powers = jnp.exp(scores - peak)
    total = jnp.sum(powers, axis=1, keepdims=True)
    weights = powers.astype(BF16)
    summed = jnp.concatenate(
        [
            functools.reduce(
                jnp.add,
                [
                    jnp.dot(
                        weights[lines[i], j * page : (j + 1) * page],
                        values[table[i, 0, j]],
                        preferred_element_type=F32,
                    )
                    for j in range(slots)
                ],
            )
            for i in range(rows)
        ],
        axis=0,
    )
    result = jnp.zeros(wide.shape, F32)
    for v in range(kinds):
        result = jnp.where(every == v, summed[:, v * LANES : (v + 1) * LANES], result)
    wide[...] = result / total
    column[...] = jnp.broadcast_to(peak + jnp.log(total), column.shape)

    width = heads_here * LANES
    at = lax.broadcasted_iota(jnp.int32, (rows, LANES), 1)
    for k in range(shards):
        shard = owner("seq", k)
        level = jnp.zeros((rows, LANES), F32)
        for x in range(heads_here):
            mine = pl.ds(k * heads_here + x, rows, stride=heads)
            result = wide[mine, :].astype(BF16)
            for copy in range(copies):
                out[shard * copies + copy, :, x * LANES : (x + 1) * LANES] = result
            level = jnp.where(at // 3 == x, column[mine, :], level)
        high, middle, low = thirds(level)
        part = lax.rem(at, 3)
        level = jnp.where(part == 0, high, jnp.where(part == 1, middle, low)).astype(BF16)
        for copy in range(copies):
            out[shard * copies + copy, :, width : width + LANES] = level
    if out.shape[2] > width + LANES:
        piece = hidden.shape[1] // shards
        for shard in range(shards):
            for copy in range(copies):
                out[shard * copies + copy, :, width + LANES :] = hidden[
                    :, shard * piece : (shard + 1) * piece
                ]


def attend(lengths, table, after, hidden, queries, keys, values, early, copies, per_kv, extra):
    shards = len(queries)
    rows, width = queries[0].shape
    total_rows = shards * width // LANES * rows
    return pl.pallas_call(
        functools.partial(attend_kernel, (copies, per_kv, shards)),
        name="attend",
        out_shape=jax.ShapeDtypeStruct((shards * copies, rows, width + LANES + extra), BF16),
        in_specs=[SMEM, SMEM, ANY] + [VMEM] * (shards + 4),
        out_specs=VMEM,
        scratch_shapes=[pltpu.VMEM((total_rows, LANES), F32)] * 2,
        compiler_params=pltpu.CompilerParams(vmem_limit_bytes=16 * MIB),
    )(lengths, table, after, hidden, *queries, keys, values, early)


def project_kernel(dims, received, weight, *refs):
    shards, piece = dims
    rest, (out, out_full, gathered, placed) = refs[:-4], refs[-4:]
    copies = received.shape[0] // shards
    rows = received.shape[1]
    width = received.shape[2] - LANES - piece
    for e in range(copies):
        levels, outputs = [], []
        for s in range(shards):
            block = received[s * copies + e].astype(F32)
            parts = block[:, width : width + LANES]
            levels.append(
                parts
                + pltpu.roll(parts, LANES - 1, 1)
                + pltpu.roll(parts, LANES - 2, 1)
            )
            outputs.append(block[:, :width])
        joint = functools.reduce(jnp.maximum, levels)
        factors = [jnp.exp(level - joint) for level in levels]
        total = functools.reduce(jnp.add, factors)
        factors = [factor / total for factor in factors]
        for x in range(width // LANES):
            span = slice(x * LANES, (x + 1) * LANES)
            value = functools.reduce(
                jnp.add,
                [
                    factor[:, 3 * x : 3 * x + 1] * output[:, span]
                    for factor, output in zip(factors, outputs)
                ],
            )
            gathered[e * rows : (e + 1) * rows, span] = value
    if piece:
        placed[...] = jnp.zeros_like(placed)
        lanes = pl.ds(pl.multiple_of(lax.axis_index("seq") * piece, piece), piece)
        for e in range(copies):
            placed[e * rows : (e + 1) * rows, lanes] = received[
                lax.axis_index("expert") * copies + e, :, width + LANES :
            ].astype(F32)
        residual = placed[...]
    else:
        residual = rest[0][...].astype(F32)
    attention = gathered[...].astype(BF16)
    result = jnp.dot(attention, weight[...], preferred_element_type=F32) + residual
    out_full[...] = result
    out[:, : result.shape[1]] = result.astype(BF16)
    if piece:
        tokens, columns = result.shape
        lanes = 2 * columns // tokens
        for i, part in enumerate(thirds(rest[0][...])[:2]):
            for r in range(tokens // 2):
                at = i * tokens // 2 + r
                out[at : at + 1, columns:] = part[:, r * lanes : (r + 1) * lanes].astype(BF16)


def project(received, weight, rest, shards, piece):
    columns = weight.shape[1]
    tokens = received.shape[0] // shards * received.shape[1]
    return pl.pallas_call(
        functools.partial(project_kernel, (shards, piece)),
        name="project",
        out_shape=[
            jax.ShapeDtypeStruct(
                (tokens, columns + (2 * columns // tokens if piece else 0)), BF16
            ),
            jax.ShapeDtypeStruct((tokens, columns), F32),
        ],
        in_specs=[VMEM] * (2 + len(rest)),
        out_specs=[VMEM] * 2,
        scratch_shapes=[
            pltpu.VMEM((tokens, weight.shape[0]), F32),
            pltpu.VMEM((tokens, columns), F32),
        ],
        compiler_params=pltpu.CompilerParams(vmem_limit_bytes=4 * MIB),
        cost_estimate=pl.CostEstimate(flops=LONG, bytes_accessed=0, transcendentals=0),
    )(received, weight, *rest)


def residual_kernel(after, gain, own, *refs):
    del after
    parts, (out, gains) = refs[:-2], refs[-2:]
    tokens, columns = own.shape
    resid = own[...]
    if gain.shape[0] == gains.shape[0]:
        gains[...] = gain[...]
    else:
        gains[owner("seq", 0)] = gain[0]
    for k, part in enumerate(parts):
        block = part[...].astype(F32)
        resid = resid + block[:, :columns]
        if part.shape[1] > columns:
            both = block[: tokens // 2, columns:] + block[tokens // 2 :, columns:]
            gains[owner("seq", k + 1)] = jnp.concatenate(
                [both[r : r + 1] for r in range(tokens // 2)], axis=1
            )
    out[...] = (resid * gains[lax.axis_index("expert")]).astype(BF16)


def residual_block(after, gain, own, parts, column_blocks):
    tokens, columns = own.shape
    return pl.pallas_call(
        residual_kernel,
        name="residual_block",
        out_shape=[
            jax.ShapeDtypeStruct((tokens, columns), BF16),
            jax.ShapeDtypeStruct((column_blocks, 1, columns), F32),
        ],
        in_specs=[ANY] + [VMEM] * (len(parts) + 2),
        out_specs=[VMEM] * 2,
        compiler_params=pltpu.CompilerParams(vmem_limit_bytes=2 * MIB),
        cost_estimate=pl.CostEstimate(flops=1000000000, bytes_accessed=0, transcendentals=0),
    )(after, gain, own, *parts)


def join_kernel(groups, *refs):
    blocks, out = refs[:-1], refs[-1]
    for k, block in enumerate(blocks):
        out[k // groups, owner("batch", k % groups)] = block[...]


def join(blocks, groups):
    return pl.pallas_call(
        functools.partial(join_kernel, groups),
        name="join",
        out_shape=jax.ShapeDtypeStruct((len(blocks) // groups, groups) + blocks[0].shape, BF16),
        in_specs=[VMEM] * len(blocks),
        out_specs=VMEM,
        compiler_params=pltpu.CompilerParams(vmem_limit_bytes=2 * MIB),
        cost_estimate=pl.CostEstimate(flops=1000000000, bytes_accessed=0, transcendentals=0),
    )(*blocks)


def terms(gains, stack, gate, up, parity):
    totals = None
    pairs, groups, _, columns = stack.shape
    for j in range(pairs):
        block = owner("expert", 2 * j + parity)
        x = jnp.concatenate([stack[j, g] for g in range(groups)], axis=0)
        plain = x.astype(F32) * (1.0 / gains[block])
        rows_of = pl.ds(pl.multiple_of(block * columns, columns), columns)
        new = (
            jnp.dot(x, gate[rows_of, :], preferred_element_type=F32),
            jnp.dot(x, up[rows_of, :], preferred_element_type=F32),
            jnp.sum(plain * plain, axis=1, keepdims=True),
        )
        totals = new if totals is None else tuple(map(jnp.add, totals, new))
    return totals


def enter_kernel(gains, stack, gate, up, early, out, squares):
    del early
    hidden = gate.shape[1]
    gate_part, up_part, square = terms(gains, stack, gate, up, 0)
    out[:, :hidden] = gate_part
    out[:, hidden:] = up_part
    squares[...] = jnp.broadcast_to(square, squares.shape)


def enter(gains, stack, gate, up, early):
    tokens = stack.shape[1] * stack.shape[2]
    return pl.pallas_call(
        enter_kernel,
        name="enter",
        out_shape=[
            jax.ShapeDtypeStruct((tokens, 2 * gate.shape[1]), F32),
            jax.ShapeDtypeStruct((tokens, LANES), F32),
        ],
        in_specs=[VMEM] * 5,
        out_specs=[VMEM] * 2,
        compiler_params=pltpu.CompilerParams(vmem_limit_bytes=28 * MIB),
        cost_estimate=pl.CostEstimate(flops=1000000, bytes_accessed=0, transcendentals=0),
    )(gains, stack, gate, up, early)


def leave_kernel(
    dims, gains, near, far, entered, squares, gain, gate, up, down, ids, routes,
    out, resid, mix, result, kept,
):
    shards, rows = dims
    choices, count = ids.shape
    line = lax.broadcasted_iota(jnp.int32, (count, count), 0)
    same = line == lax.broadcasted_iota(jnp.int32, (count, count), 1)
    at = lax.broadcasted_iota(jnp.int32, mix.shape, 1)
    shares = jnp.zeros(mix.shape, F32)
    for k in range(choices):
        name = jnp.sum(jnp.where(same, ids[k : k + 1, :], 0), axis=1, keepdims=True)
        share = jnp.sum(jnp.where(same, routes[k : k + 1, :], 0.0), axis=1, keepdims=True)
        shares = shares + jnp.where(at == name, share, 0.0)
    mix[...] = shares
    seq, own, group = [lax.axis_index(name) for name in ("seq", "expert", "batch")]
    pairs, groups, tokens, columns = near.shape
    column_blocks = 2 * pairs
    features = column_blocks * columns
    width = features // shards
    hidden = down.shape[0]
    gate_part, up_part, square = terms(gains, far, gate, up, 1)
    scale = lax.rsqrt((squares[:, :1] + square) / features + EPS)
    gate_part = (entered[:, :hidden] + gate_part) * scale
    up_part = (entered[:, hidden:] + up_part) * scale
    act = (gate_part / (1.0 + jnp.exp(-gate_part)) * up_part).astype(BF16)
    result[...] = jnp.dot(act, down[...], preferred_element_type=F32)
    for s in range(shards):
        for e in range(column_blocks):
            for g in range(groups):
                at = g * tokens + e * rows
                out[(s * column_blocks + e) * groups + g] = result[
                    at : at + rows, s * width : (s + 1) * width
                ].astype(BF16)
    first = seq * width
    lanes = pl.ds(pl.multiple_of(lax.rem(first, columns), width), width)
    for k in range(column_blocks):

        @pl.when(first // columns == owner("expert", k))
        def _(k=k):
            kept[...] = (far if k % 2 else near)[k // 2, group].astype(F32)

    for e in range(column_blocks):

        @pl.when(own == e)
        def _(e=e):
            resid[...] = kept[e * rows : (e + 1) * rows, lanes] / gain[...]


def leave(gains, near, far, entered, squares, gain, gate, up, down, ids, routes, shards, rows):
    pairs, groups, tokens, columns = near.shape
    features = down.shape[1]
    return pl.pallas_call(
        functools.partial(leave_kernel, (shards, rows)),
        name="leave",
        out_shape=[
            jax.ShapeDtypeStruct((2 * pairs * groups * shards, rows, features // shards), BF16),
            jax.ShapeDtypeStruct((rows, features // shards), F32),
            jax.ShapeDtypeStruct((rows, LANES), F32),
        ],
        in_specs=[VMEM] * 11,
        out_specs=[VMEM] * 3,
        scratch_shapes=[
            pltpu.VMEM((groups * tokens, features), F32),
            pltpu.VMEM((tokens, columns), F32),
        ],
        compiler_params=pltpu.CompilerParams(vmem_limit_bytes=8 * MIB),
    )(
        gains, near, far, entered, squares, gain,
        in_vmem(gate), in_vmem(up), in_vmem(down), ids, routes,
    )


def finish_kernel(dims, mix, returned, resid, out):
    shards, experts, groups = dims
    total = resid[...]
    for e in range(experts):
        term = None
        for s in range(shards):
            for g in range(groups):
                part = returned[(s * experts + e) * groups + g].astype(F32)
                term = part if term is None else term + part
        total = total + mix[:, e : e + 1] * term
    out[...] = total.astype(BF16)


def finish(mix, returned, resid, dims):
    return pl.pallas_call(
        functools.partial(finish_kernel, dims),
        name="finish",
        out_shape=jax.ShapeDtypeStruct(resid.shape, BF16),
        in_specs=[VMEM] * 3,
        out_specs=VMEM,
        compiler_params=pltpu.CompilerParams(vmem_limit_bytes=4 * MIB),
    )(mix, returned, resid)


def per_device(
    hidden_state,
    queries,
    page_table,
    lengths,
    paged_keys,
    paged_values,
    out_weight,
    norm_gain,
    expert_ids,
    route_weights,
    expert_gate,
    expert_up,
    expert_down,
):
    shards = lax.axis_size("seq")
    experts = lax.axis_size("expert")
    groups = lax.axis_size("batch")
    rows = hidden_state.shape[0]
    columns = out_weight.shape[1]
    kv_heads = paged_keys.shape[3] // LANES
    per_kv = shards * queries.shape[1] // LANES // kv_heads
    own_gain = norm_gain[None, :]
    own_features = hidden_state.shape[1]

    piece = own_features // shards
    if own_features == columns and piece % LANES == 2 * columns % (experts * rows * LANES) == 0:
        rest = [own_gain]
        gain = own_gain[None]
    else:
        piece = 0
        everything = lax.all_gather(hidden_state, "expert", axis=0, tiled=True)
        everything = lax.all_gather(everything, "seq", axis=1, tiled=True)
        first = lax.axis_index("expert") * columns
        block = lax.dynamic_slice_in_dim(everything, first, columns, 1)
        gain = lax.all_gather(norm_gain, "seq", axis=0, tiled=True)
        gain = gain.reshape(experts, 1, columns)
        rest = [jnp.where(lax.axis_index("seq") == 0, block, 0)]

    partials = attend(
        lengths,
        page_table,
        pause(in_hbm(queries)),
        hidden_state,
        exchange(queries, "seq"),
        paged_keys[0],
        paged_values[0],
        out_weight,
        experts,
        per_kv,
        piece,
    )
    received = lax.all_to_all(
        partials, ("seq", "expert"), split_axis=0, concat_axis=0, tiled=True
    )
    projected, own = project(received, out_weight, rest, shards, piece)

    parts = exchange(projected, "seq")[1:]
    block, gains = residual_block(pause(projected), gain, own, parts, experts)
    gate, up, down = expert_gate[0], expert_up[0], expert_down[0]

    routes = [j * groups + k for j in range(0, experts, 2) for k in range(groups)]
    devices = range(experts * groups)
    near = join(
        [block]
        + [
            lax.ppermute(block, ("expert", "batch"), [(i, i ^ k) for i in devices])
            for k in routes[1:]
        ],
        groups,
    )
    far = lax.ppermute(near, "expert", [(i, i ^ 1) for i in range(experts)])
    entered, squares = enter(gains, near, gate, up, down)
    outputs, resid, mix = leave(
        gains, near, far, entered, squares, own_gain, gate, up, down,
        expert_ids.T, route_weights.T, shards, rows,
    )
    returned = lax.all_to_all(
        outputs, ("seq", "expert", "batch"), split_axis=0, concat_axis=0, tiled=True
    )
    return finish(mix, returned, resid, (shards, experts, groups))


def solution(mesh):
    in_specs = (
        P(("batch", "expert"), "seq"),
        P(("batch", "expert"), "seq"),
        P(("batch", "expert"), "seq", None),
        P(("batch", "expert")),
        P(("batch", "expert"), "seq", None, None),
        P(("batch", "expert"), "seq", None, None),
        P("seq", "expert"),
        P("seq"),
        P(("batch", "expert"), None),
        P(("batch", "expert"), None),
        P("expert", None, ("seq", "batch")),
        P("expert", None, ("seq", "batch")),
        P("expert", ("seq", "batch"), None),
    )
    out_specs = P(("batch", "expert"), "seq")
    return jax.shard_map(
        per_device, mesh=mesh, in_specs=in_specs, out_specs=out_specs, check_vma=False
    )
```
